32 devices in a mesh: groups: 2 (over y), seq: 4 (over x, core), role: 4 (over z).
Axes of the slice: x: 2, y: 2, z: 4, core: 2. Of those that a mesh axis runs over, the one named last changes fastest.
Arguments:
- query_rows: bfloat16 [8, 256, 4096], P('groups', 'seq', 'role'), parts along dimension 0, may hold values from -6 to 6
- encoded_key_rows: bfloat16 [8, 256, 512], P('groups', ('seq', 'role')), parts along dimension 0, may hold values from -6 to 6
- value_matrix_rows: bfloat16 [8, 256, 512], P('groups', ('seq', 'role')), parts along dimension 0, may hold values from -6 to 6
- output_weight: bfloat16 [4096, 2048], P('role', 'seq'), may hold values from -0.09375 to 0.09375
- residual: bfloat16 [8, 256, 2048], P(('groups', 'role'), 'seq'), parts along dimension 0, may hold values from -7.5 to 7.5
- norm_gain: float32 [2048], replicated, may hold values from 0.5 to 1.5
- route_experts: int32 [8, 256, 8], P(('groups', 'role'), 'seq'), parts along dimension 0, may hold values from 0 to 15, all different within a row; in each aligned block of 64 rows (0 to 63, 64 to 127, ..., all dimensions but the last counted through in order) at most 33 rows name the same one
- route_gates: float32 [8, 256, 8], P(('groups', 'role'), 'seq'), parts along dimension 0, may hold values from 0.05 to 0.3
- gate_weight: bfloat16 [16, 2048, 768], P(('seq', 'role')), may hold values from -0.125 to 0.125
- up_weight: bfloat16 [16, 2048, 768], P(('seq', 'role')), may hold values from -0.125 to 0.125
- down_weight: bfloat16 [16, 768, 2048], P(('seq', 'role')), may hold values from -0.21875 to 0.21875
Outputs:
- layer_output: bfloat16 [8, 256, 2048], P(('groups', 'role'), 'seq'), parts along dimension 0
The draws below stay inside these ranges and needn't reach their ends.
There are 2 independent parts, one for each index of `groups`. The reference program is written for one: setup_inputs(seed, part) draws one part's arguments, and reference() takes and returns one part's arrays. A program takes and returns all parts, laid end to end along the dimension named above; an argument that names none is the same for every part. Nothing has to cross between parts.
Inputs may be any that keep to these rules, and one draw needn't show every extreme that they name: `route_experts`: each token names 8 different experts. Within the 64 positions of one sequence that one index of seq holds, no expert is named by more than 33 routes, and in every draw some expert is named by exactly 33 routes in some such block.
All inputs are finite; a program needn't handle non-finite values.
Results may differ from the reference program's by a relative error of at most 0.014.
Values may be sent and summed in bfloat16 or wider, within the bound.
A program may use at most 128 MiB of HBM per device.

```python
import math
import jax
import jax.numpy as jnp
import numpy as np
from jax import lax

D = 2048
FF = 768
QUERY_HEADS = 32
KEY_VALUE_HEADS = 4
HEAD_WIDTH = 128
TOPK = 8
SEQ_TOK = 64
EXPERTS = 16
SEQUENCE_LENGTH = 256
BATCH_SEQUENCES = 4
HPD = 8
CAP = 33
N_SEQ = 4
N_ROLE = 4


def draw_query_rows(key, part):
    value_entries = jnp.clip(1.5 * jax.random.normal(jax.random.fold_in(key, 11), (BATCH_SEQUENCES, SEQUENCE_LENGTH, QUERY_HEADS * HEAD_WIDTH), jnp.float32), -6.0, 6.0)
    return value_entries.astype(jnp.bfloat16)


def draw_encoded_key_rows(key, part):
    value_entries = jnp.clip(1.5 * jax.random.normal(jax.random.fold_in(key, 12), (BATCH_SEQUENCES, SEQUENCE_LENGTH, KEY_VALUE_HEADS * HEAD_WIDTH), jnp.float32), -6.0, 6.0)
    return value_entries.astype(jnp.bfloat16)


def draw_residual(key, part):
    random_splits = jax.random.split(jax.random.fold_in(key, 13), 3)
    row_scale = jnp.exp(jax.random.uniform(random_splits[1], (BATCH_SEQUENCES, SEQUENCE_LENGTH, 1), jnp.float32, math.log(0.25), math.log(2.5)))
    column_scale = jnp.exp(jax.random.uniform(random_splits[0], (D,), jnp.float32, math.log(0.1), 0.0))
    noise_rows = jnp.clip(jax.random.normal(random_splits[2], (BATCH_SEQUENCES, SEQUENCE_LENGTH, D), jnp.float32), -3.0, 3.0)
    return (noise_rows * column_scale * row_scale).astype(jnp.bfloat16)


def block_scale(stream_key, dims, pieces, least, largest):
    gain, own = 1.0, jax.random.fold_in(stream_key, 6)
    for axis_at, shards_of in pieces:
        draws = jnp.exp(jax.random.uniform(jax.random.fold_in(own, axis_at), (shards_of,), jnp.float32, least / len(pieces), largest / len(pieces)))
        gain = gain * jnp.repeat(draws, dims[axis_at] // shards_of).reshape([-1 if axis == axis_at else 1 for axis in range(len(dims))])
    return gain


def shared_out(key, own, number, rows, amount, top, most, skew):
    sequence = jax.random.permutation(key, amount)
    packed, usual = load_shares(amount, rows * top, most, skew, True), load_shares(amount, rows * top, most, skew, False)
    places = jnp.arange(amount)

    def named(sizes, turn):
        used = int((sizes > 0).sum())
        fixed = max(1, used // 4)
        shifted = fixed + (places - fixed + turn * (used - fixed)) % max(1, amount - fixed)
        return jnp.zeros((amount,), jnp.int32).at[sequence[jnp.where(places < fixed, places, shifted)]].set(jnp.asarray(sizes, jnp.int32))

    sizes = jnp.where(number % 4 == 0, named(packed, number // 4), named(usual, number - number // 4 - 1))
    mixed = jax.random.permutation(jax.random.fold_in(own, 3), amount)
    source_of, receiver = mixed[0:amount // 2 * 2:2], mixed[1:amount // 2 * 2:2]
    room = jnp.minimum(sizes[source_of] - 1, most - sizes[receiver]) // 2
    room = jnp.where((source_of == sequence[0]) | (receiver == sequence[0]) | (sizes[receiver] == 0), 0, jnp.maximum(room, 0))
    shifted = jax.random.randint(jax.random.fold_in(own, 4), (amount // 2,), 0, 1 << 20) % (room + 1)
    sizes = sizes.at[source_of].add(-shifted).at[receiver].add(shifted)
    members = jnp.searchsorted(jnp.cumsum(sizes), jnp.arange(rows * top), side="right").astype(jnp.int32)
    grid = members.reshape(top, rows).T
    grid = grid[jax.random.permutation(jax.random.fold_in(own, 1), rows)]
    turn = jax.random.randint(jax.random.fold_in(own, 2), (rows, 1), 0, top)
    return jnp.take_along_axis(grid, (jnp.arange(top)[None, :] + turn) % top, axis=1)


def load_shares(amount, total, bound, slope, full):
    weights = [(1 << 20) // math.isqrt(grade ** slope) + 1 for grade in range(1, amount + 1)]
    largest = bound if full else min(bound, max(-(-total // amount), total * weights[0] // sum(weights)))
    least = 1 if total - largest >= amount - 1 else 0
    holding, surplus = [largest] + [least] * (amount - 1), total - largest - least * (amount - 1)
    while surplus > 0:
        movable = [i for i in range(1, amount) if holding[i] < largest] or [i for i in range(1, amount) if holding[i] < bound]
        whole, left = sum([weights[i] for i in movable]), surplus
        for i in movable:
            addition = min(bound - holding[i], max(1, left * weights[i] // whole), surplus)
            holding[i] = holding[i] + addition
            surplus = surplus - addition
    return np.array(holding)


def normal_values(rng, dims, deviation, bound, cuts=(), kind=jnp.bfloat16):
    loudness = block_scale(rng, dims, cuts, -0.22, 0.18) if cuts else 1.0
    drawn = jax.random.normal(rng, dims, jnp.float32) * deviation * loudness
    return jnp.minimum(jnp.maximum(drawn, -bound), bound).astype(kind)


def setup_inputs(seed: int = 0, part: int = 0) -> dict:
    key_of = jax.random.split(jax.random.key(seed), 12)
    part_keys = jax.random.split(jax.random.fold_in(key_of[11], part), 12)
    query_rows = draw_query_rows(jax.random.fold_in(jax.random.fold_in(key_of[11], part), 71), part)
    encoded_key_rows = draw_encoded_key_rows(jax.random.fold_in(jax.random.fold_in(key_of[11], part), 71), part)
    value_matrix_rows = normal_values(part_keys[2], (BATCH_SEQUENCES, SEQUENCE_LENGTH, KEY_VALUE_HEADS * HEAD_WIDTH), 1.0, 6.0, ((1, 16),))
    output_weight = normal_values(key_of[3], (QUERY_HEADS * HEAD_WIDTH, D), (QUERY_HEADS * HEAD_WIDTH) ** -0.5, 0.09375, ((0, 4), (1, 4)))
    residual = draw_residual(jax.random.fold_in(jax.random.fold_in(key_of[11], part), 71), part)
    norm_gain = jnp.clip(1.0 + 0.1 * jax.random.normal(key_of[5], (D,), jnp.float32), 0.5, 1.5)
    route_experts_keys = jax.random.split(jax.random.fold_in(part_keys[6], 1), BATCH_SEQUENCES * SEQUENCE_LENGTH // SEQ_TOK)
    route_experts_turns = jax.random.permutation(jax.random.fold_in(part_keys[6], 3), BATCH_SEQUENCES * SEQUENCE_LENGTH // SEQ_TOK)
    route_experts = jax.vmap(lambda own, number: shared_out(jax.random.fold_in(part_keys[6], 2), own, number, SEQ_TOK, EXPERTS, TOPK, CAP, 1))(route_experts_keys, route_experts_turns).reshape((BATCH_SEQUENCES, SEQUENCE_LENGTH, TOPK))
    route_gates = jnp.clip(0.05 + 0.25 * jax.random.uniform(part_keys[7], (BATCH_SEQUENCES, SEQUENCE_LENGTH, TOPK), jnp.float32) ** block_scale(part_keys[7], (BATCH_SEQUENCES, SEQUENCE_LENGTH, TOPK), ((0, 4), (1, 4)), -0.2, 0.2), 0.05, 0.3)
    gate_weight = normal_values(key_of[8], (EXPERTS, D, FF), D ** -0.5, 0.125, ((0, 16),))
    up_weight = normal_values(key_of[9], (EXPERTS, D, FF), D ** -0.5, 0.125, ((0, 16),))
    down_weight = normal_values(key_of[10], (EXPERTS, FF, D), FF ** -0.5, 0.21875, ((0, 16),))
    return dict(query_rows=query_rows, encoded_key_rows=encoded_key_rows, value_matrix_rows=value_matrix_rows, output_weight=output_weight, residual=residual, norm_gain=norm_gain, route_experts=route_experts, route_gates=route_gates, gate_weight=gate_weight, up_weight=up_weight, down_weight=down_weight)


epsilon = 1e-06
masked_score = -1e+30

def attend_head(query_head, key_head, value_head):
    length = query_head.shape[0]
    scores = jnp.dot(query_head.astype(jnp.float32), key_head.astype(jnp.float32).T, precision=lax.Precision.HIGHEST) * HEAD_WIDTH ** (-0.5)
    positions = jnp.arange(length, dtype=jnp.int32)
    causal = positions[None, :] <= positions[:, None]
    scores = jnp.where(causal, scores, masked_score)
    row_peak = lax.optimization_barrier(jnp.max(scores, axis=1, keepdims=True))
    weights = jnp.exp(scores - row_peak)
    totals = lax.optimization_barrier(jnp.sum(weights, axis=1, keepdims=True))
    rounded = weights.astype(jnp.bfloat16)
    mixed_rows = jnp.dot(rounded.astype(jnp.float32), value_head.astype(jnp.float32), precision=lax.Precision.HIGHEST) / totals
    return mixed_rows.astype(jnp.bfloat16)

def reference(query_rows, encoded_key_rows, value_matrix_rows, output_weight, residual, norm_gain, route_experts, route_gates, gate_weight, up_weight, down_weight):
    query_group_width = QUERY_HEADS // KEY_VALUE_HEADS
    heads_query = query_rows.reshape(BATCH_SEQUENCES, SEQUENCE_LENGTH, QUERY_HEADS, HEAD_WIDTH)
    key_per_head = encoded_key_rows.reshape(BATCH_SEQUENCES, SEQUENCE_LENGTH, KEY_VALUE_HEADS, HEAD_WIDTH)
    value_per_head = value_matrix_rows.reshape(BATCH_SEQUENCES, SEQUENCE_LENGTH, KEY_VALUE_HEADS, HEAD_WIDTH)

    def one_pair(pair_index):
        batch_index = pair_index // QUERY_HEADS
        head_index = pair_index % QUERY_HEADS
        kv_index = head_index // query_group_width
        return attend_head(heads_query[batch_index, :, head_index], key_per_head[batch_index, :, kv_index], value_per_head[batch_index, :, kv_index])
    attended = lax.map(one_pair, jnp.arange(BATCH_SEQUENCES * QUERY_HEADS, dtype=jnp.int32))
    attended = attended.reshape(BATCH_SEQUENCES, QUERY_HEADS, SEQUENCE_LENGTH, HEAD_WIDTH).transpose(0, 2, 1, 3).reshape(BATCH_SEQUENCES, SEQUENCE_LENGTH, QUERY_HEADS * HEAD_WIDTH)
    grouped_weight = output_weight.astype(jnp.float32).reshape(N_ROLE, HPD * HEAD_WIDTH, D)

    def project(sequence_rows):
        split_rows = sequence_rows.astype(jnp.float32).reshape(SEQUENCE_LENGTH, N_ROLE, HPD * HEAD_WIDTH)
        partials = jnp.einsum('lgk,gkd->lgd', split_rows, grouped_weight, precision=lax.Precision.HIGHEST)
        partials = lax.optimization_barrier(partials.astype(jnp.bfloat16))
        return lax.optimization_barrier(jnp.sum(partials.astype(jnp.float32), axis=1))
    projected = lax.map(project, attended)
    hidden = residual.astype(jnp.float32) + projected
    variance = lax.optimization_barrier(jnp.mean(hidden * hidden, axis=-1, keepdims=True))
    normed = (hidden * lax.rsqrt(variance + epsilon) * norm_gain).astype(jnp.bfloat16)
    tokens = BATCH_SEQUENCES * SEQUENCE_LENGTH
    flat_inputs = normed.reshape(tokens, D)
    flat_ids = route_experts.reshape(tokens * TOPK)
    flat_gates = route_gates.reshape(tokens * TOPK)
    most_rows = CAP * N_SEQ * N_ROLE

    def one_expert(running, inputs):
        gate_matrix, up_matrix, down_matrix, expert = inputs
        chosen = flat_ids == expert
        picked = jnp.nonzero(chosen, size=most_rows, fill_value=0)[0]
        listed = jnp.sum(chosen.astype(jnp.int32))
        valid = jnp.arange(most_rows, dtype=jnp.int32) < listed
        token_index = picked // TOPK
        row_block = flat_inputs[token_index].astype(jnp.float32)
        gate_hidden = jnp.dot(row_block, gate_matrix.astype(jnp.float32), precision=lax.Precision.HIGHEST)
        up_hidden = jnp.dot(row_block, up_matrix.astype(jnp.float32), precision=lax.Precision.HIGHEST)
        activated = (jax.nn.silu(gate_hidden) * up_hidden).astype(jnp.bfloat16)
        expert_out = jnp.dot(activated.astype(jnp.float32), down_matrix.astype(jnp.float32), precision=lax.Precision.HIGHEST)
        expert_out = lax.optimization_barrier(expert_out.astype(jnp.bfloat16))
        weight = jnp.where(valid, flat_gates[picked], 0.0)
        running = running.at[token_index].add(weight[:, None] * expert_out.astype(jnp.float32))
        return (running, None)
    start_sum = jnp.zeros((tokens, D), jnp.float32)
    expert_sum, unused = lax.scan(one_expert, start_sum, (gate_weight, up_weight, down_weight, jnp.arange(EXPERTS, dtype=jnp.int32)))
    return (hidden + expert_sum.reshape(BATCH_SEQUENCES, SEQUENCE_LENGTH, D)).astype(jnp.bfloat16)
```

```python
from functools import partial

import jax
import jax.numpy as jnp
from jax import lax
from jax.experimental import pallas as pl
from jax.experimental.pallas import tpu as pltpu
from jax.sharding import PartitionSpec as P

D = 2048
QUERY_HEADS = 32
KEY_VALUE_HEADS = 4
HEAD_WIDTH = 128
TOPK = 8


epsilon = 1e-06
masked_score = -1e30


def score_block(queries, every_key, query_position, block_start, block_width, score_scale):
    keys_part = lax.slice_in_dim(every_key, block_start, block_start + block_width, axis=0)
    raw_scores = (
        jnp.einsum("qhd,kd->hqk", queries, keys_part, preferred_element_type=jnp.float32)
        * score_scale
    )
    key_position = block_start + jnp.arange(block_width, dtype=jnp.int32)
    return jnp.where(
        key_position[None, None, :] <= query_position[None, :, None], raw_scores, masked_score
    )


def value_block(rounded, every_value, block_start, block_width):
    prob_block = lax.slice_in_dim(rounded, block_start, block_start + block_width, axis=2)
    values_part = lax.slice_in_dim(every_value, block_start, block_start + block_width, axis=0)
    return jnp.einsum("hqk,kd->qhd", prob_block, values_part, preferred_element_type=jnp.float32)


def shards(
    query_rows,
    encoded_key_rows,
    value_matrix_rows,
    output_weight,
    residual,
    norm_gain,
    route_experts,
    route_gates,
    gate_weight,
    up_weight,
    down_weight,
):
    seq_count = lax.axis_size("seq")
    role_count = lax.axis_size("role")
    seq_index = lax.axis_index("seq")
    role_index = lax.axis_index("role")
    batch_count = query_rows.shape[0]
    local_length = query_rows.shape[1]
    local_heads = query_rows.shape[2] // HEAD_WIDTH
    full_length = local_length * seq_count
    query_group_width = QUERY_HEADS // KEY_VALUE_HEADS
    head_pick = role_index * local_heads // query_group_width
    role_keys, role_values = (
        lax.all_gather(encoded_key_rows, "role", axis=1, tiled=True),
        lax.all_gather(value_matrix_rows, "role", axis=1, tiled=True),
    )
    head_keys = lax.dynamic_slice_in_dim(role_keys, head_pick * HEAD_WIDTH, HEAD_WIDTH, 2)
    head_values = lax.dynamic_slice_in_dim(role_values, head_pick * HEAD_WIDTH, HEAD_WIDTH, 2)
    whole_keys, whole_values, whole_proj = (
        lax.all_gather(head_keys, "seq", axis=1, tiled=True),
        lax.all_gather(head_values, "seq", axis=1, tiled=True),
        lax.all_gather(output_weight, "seq", axis=1, tiled=True),
    )
    key_width = full_length // 8
    score_scale = HEAD_WIDTH ** (-0.5)
    query_position = seq_index * local_length + jnp.arange(local_length, dtype=jnp.int32)
    last_needed = (seq_index + 1) * local_length

    def one_sequence(operands):
        own_queries, every_key, every_value = operands
        queries = own_queries.reshape(local_length, local_heads, HEAD_WIDTH)
        pieces = []
        for number in range(8):
            block_start = number * key_width
            compute = partial(
                score_block, queries, every_key, query_position, block_start, key_width, score_scale
            )
            skipped = partial(
                jnp.full, (local_heads, local_length, key_width), masked_score, jnp.float32
            )
            pieces.append(lax.cond(block_start < last_needed, compute, skipped))
        scores = jnp.concatenate(pieces, axis=2)
        row_peak = jnp.max(scores, axis=2, keepdims=True)
        weights = jnp.exp(scores - row_peak)
        totals = jnp.sum(weights, axis=2, keepdims=True)
        rounded = weights.astype(jnp.bfloat16)
        mixed_rows = jnp.zeros((local_length, local_heads, HEAD_WIDTH), jnp.float32)
        for number in range(8):
            block_start = number * key_width
            product = partial(value_block, rounded, every_value, block_start, key_width)
            nothing = partial(jnp.zeros, (local_length, local_heads, HEAD_WIDTH), jnp.float32)
            mixed_rows = mixed_rows + lax.cond(block_start < last_needed, product, nothing)
        attended = (mixed_rows / totals.transpose(1, 0, 2)).astype(jnp.bfloat16)
        return attended.reshape(local_length, local_heads * HEAD_WIDTH)

    attended = lax.map(one_sequence, (query_rows, whole_keys, whole_values))
    flat_attended = attended.reshape(batch_count * local_length, local_heads * HEAD_WIDTH)
    projected = lax.psum_scatter(
        jnp.dot(flat_attended, whole_proj, preferred_element_type=jnp.float32).astype(jnp.bfloat16),
        "role",
        scatter_dimension=0,
        tiled=True,
    ).astype(jnp.float32)
    hidden = residual[0].astype(jnp.float32) + projected
    variance = jnp.mean(hidden * hidden, axis=-1, keepdims=True)
    normed = (hidden * lax.rsqrt(variance + epsilon) * norm_gain).astype(jnp.bfloat16)
    expert_ids = route_experts.reshape(-1)
    gate_values = route_gates.reshape(-1)
    experts_local = gate_weight.shape[0]
    device_count = seq_count * role_count
    expert_count = experts_local * device_count
    assign = expert_ids.shape[0]
    capacity = assign // expert_count + 1
    onehot = (expert_ids[:, None] == jnp.arange(expert_count, dtype=jnp.int32)[None, :]).astype(
        jnp.int32
    )
    earlier = jnp.cumsum(onehot, axis=0) - onehot
    slot_rank = jnp.sum(earlier * onehot, axis=1)
    slot_index = expert_ids * capacity + slot_rank
    source_token = jnp.arange(assign, dtype=jnp.int32) // TOPK
    slot_token = jnp.zeros((expert_count * capacity,), jnp.int32).at[slot_index].set(source_token)
    slot_used = jnp.zeros((expert_count * capacity,), jnp.bfloat16).at[slot_index].set(1.0)
    outgoing = (normed[slot_token] * slot_used[:, None]).reshape(
        device_count, experts_local, capacity, D
    )
    incoming = lax.all_to_all(outgoing, ("seq", "role"), split_axis=0, concat_axis=0, tiled=True)
    gate_hidden = jnp.einsum(
        "sjcd,jdf->sjcf", incoming, gate_weight, preferred_element_type=jnp.float32
    )
    up_hidden = jnp.einsum(
        "sjcd,jdf->sjcf", incoming, up_weight, preferred_element_type=jnp.float32
    )
    activated = (jax.nn.silu(gate_hidden) * up_hidden).astype(jnp.bfloat16)
    returned = lax.all_to_all(
        jnp.einsum(
            "sjcf,jfd->sjcd", activated, down_weight, preferred_element_type=jnp.float32
        ).astype(jnp.bfloat16),
        ("seq", "role"),
        split_axis=0,
        concat_axis=0,
        tiled=True,
    )
    gathered = returned.reshape(expert_count * capacity, D)[slot_index]
    weighted = gathered.astype(jnp.float32) * gate_values[:, None]
    expert_sum = jnp.sum(weighted.reshape(-1, TOPK, D), axis=1)
    return (hidden + expert_sum).astype(jnp.bfloat16).reshape(residual.shape)


MESH = pl.DeviceIdType.MESH
LANES = 128


def aligned(index, size):
    return pl.ds(pl.multiple_of(index * size, size), size)


def layer_kernel(
    roles,
    seqs,
    q_hbm,
    k_hbm,
    v_hbm,
    wo_hbm,
    res_hbm,
    gain_hbm,
    ids_hbm,
    gates_hbm,
    gw_hbm,
    uw_hbm,
    dw_hbm,
    out_ref,
    q,
    kv,
    wo,
    res,
    gain,
    ids,
    gates,
    gw,
    uw,
    dw,
    att,
    part,
    part_in,
    hid,
    tok,
    act,
    y,
    y_core,
    y_x,
    y_role,
    load_sem,
    own_sem,
    kv1_s,
    kv1_r,
    kv2_s,
    kv2_r,
    wo_s,
    wo_r,
    pr_s,
    pr_r,
    tz_s,
    tz_r,
    tx_s,
    tx_r,
    tc_s,
    tc_r,
    yc_s,
    yc_r,
    yx_s,
    yx_r,
    yz_s,
    yz_r,
):
    s = lax.axis_index("seq")
    r = lax.axis_index("role")
    mate = s + 1 - 2 * (s % 2)
    side = (s + 2) % 4
    far = mate + 2 - 4 * (mate // 2)
    batch, rows, width = q.shape
    heads = width // HEAD_WIDTH
    own_keys = k_hbm.shape[1]
    full = rows * seqs
    cols = wo.shape[2]
    offs = (2, 1, 3)

    def remote(src, dst, ssem, rsem, device):
        return pltpu.make_async_remote_copy(
            src_ref=src,
            dst_ref=dst,
            send_sem=ssem,
            recv_sem=rsem,
            device_id=device,
            device_id_type=MESH,
        )

    def to_role(off):
        return {"role": (r + off) % roles}

    barrier = pltpu.get_barrier_semaphore()
    for off in offs:
        pl.semaphore_signal(barrier, inc=1, device_id=to_role(off), device_id_type=MESH)
    for peer in (mate, side):
        pl.semaphore_signal(barrier, inc=1, device_id={"seq": peer}, device_id_type=MESH)

    loads = [
        pltpu.make_async_copy(a, b, load_sem.at[i])
        for i, (a, b) in enumerate(
            (
                (q_hbm, q),
                (res_hbm, res),
                (gain_hbm, gain),
                (ids_hbm, ids),
                (gates_hbm, gates),
                (wo_hbm, wo.at[s]),
                (gw_hbm, gw),
                (uw_hbm, uw),
                (dw_hbm, dw),
            )
        )
    ]
    pair = (k_hbm, v_hbm)

    def kv_spot(t, seq, role):
        return kv.at[t, :, aligned(seq * roles + role, own_keys), :]

    owns = [
        pltpu.make_async_copy(
            pair[t].at[:, :, aligned(r, HEAD_WIDTH)], kv_spot(t, s, r), own_sem.at[t]
        )
        for t in range(2)
    ]
    for copy in owns + loads[:6]:
        copy.start()
    pl.semaphore_wait(barrier, roles - 1 + 2)

    def kv1(t, off):
        return remote(
            pair[t].at[:, :, aligned((r + off) % roles, HEAD_WIDTH)],
            kv_spot(t, s, r),
            kv1_s.at[t, off],
            kv1_r.at[t, off],
            to_role(off),
        )

    def kv1_in(t, off):
        source = (r + roles - off) % roles
        return remote(
            pair[t].at[:, :, aligned(r, HEAD_WIDTH)],
            kv_spot(t, s, source),
            kv1_s.at[t, off],
            kv1_r.at[t, off],
            to_role(off),
        )

    for off in offs:
        for t in range(2):
            kv1(t, off).start()
    for copy in loads[6:]:
        copy.start()

    def kv2(t, path, seq, target):
        spot = kv.at[t, :, aligned(seq, rows), :]
        return remote(spot, spot, kv2_s.at[t, path], kv2_r.at[t, path], {"seq": target})

    def wo2(path, seq, target):
        return remote(wo.at[seq], wo.at[seq], wo_s.at[path], wo_r.at[path], {"seq": target})

    for copy in owns:
        copy.wait()
    for off in offs:
        for t in range(2):
            kv1_in(t, off).wait_recv()
    for t in range(2):
        kv2(t, 1, s, side).start()
        kv2(t, 0, s, mate).start()
    loads[5].wait()
    wo2(1, s, side).start()
    wo2(0, s, mate).start()

    for copy in loads[:5]:
        copy.wait()
    lane = lax.broadcasted_iota(jnp.int32, (rows, LANES), 1)
    table = jnp.zeros((rows, LANES), jnp.float32)
    for k in range(ids.shape[2]):
        chosen = lane % (LANES // 2) == ids[0, :, k : k + 1]
        table = table + jnp.where(chosen, gates[0, :, k : k + 1], 0.0)
    high = table.astype(jnp.bfloat16)
    low = (table - high.astype(jnp.float32)).astype(jnp.bfloat16)
    depth = hid.shape[1]
    tok[r, aligned(s, rows), depth : depth + LANES] = jnp.where(
        lane < LANES // 2, high.astype(jnp.float32), low.astype(jnp.float32)
    ).astype(jnp.bfloat16)

    for t in range(2):
        kv2(t, 1, side, side).wait_recv()
        kv2(t, 2, side, mate).start()
    for t in range(2):
        kv2(t, 0, mate, mate).wait_recv()
        kv2(t, 2, far, mate).wait_recv()

    query_row = s * rows + lax.broadcasted_iota(jnp.int32, (rows, full), 0)
    allowed = lax.broadcasted_iota(jnp.int32, (rows, full), 1) <= query_row

    def attend(b, carry):
        keys, values = kv[0, b], kv[1, b]
        for h in range(heads):
            head = pl.ds(h * HEAD_WIDTH, HEAD_WIDTH)
            scores = lax.dot_general(
                q[b, :, head],
                keys,
                (((1,), (1,)), ((), ())),
                preferred_element_type=jnp.float32,
            ) * (HEAD_WIDTH**-0.5)
            scores = jnp.where(allowed, scores, masked_score)
            weights = jnp.exp(scores - jnp.max(scores, axis=1, keepdims=True))
            totals = jnp.sum(weights, axis=1, keepdims=True)
            mixed = jnp.dot(
                weights.astype(jnp.bfloat16), values, preferred_element_type=jnp.float32
            )
            att[aligned(b, rows), head] = (mixed / totals).astype(jnp.bfloat16)
        return carry

    lax.fori_loop(0, batch, attend, 0)

    def pr(j, off):
        return remote(
            part.at[j, aligned((r + off) % roles, rows), :],
            part_in.at[j, off],
            pr_s.at[j, off],
            pr_r.at[j, off],
            to_role(off),
        )

    def project(j):
        part[j] = jnp.dot(att[...], wo[j], preferred_element_type=jnp.float32).astype(
            jnp.bfloat16
        )
        for off in offs:
            pr(j, off).start()

    project(s)
    wo2(0, mate, mate).wait_recv()
    project(mate)
    wo2(1, side, side).wait_recv()
    wo2(2, side, mate).start()
    project(side)
    wo2(2, far, mate).wait_recv()
    project(far)

    square = jnp.zeros((rows, 1), jnp.float32)
    for j in range(seqs):
        block = pl.ds(j * cols, cols)
        total = part[j, aligned(r, rows), :].astype(jnp.float32)
        for off in offs:
            pr(j, off).wait_recv()
            total = total + part_in[j, off].astype(jnp.float32)
        hidden = res[0, :, block].astype(jnp.float32) + total
        hid[:, block] = hidden
        square = square + jnp.sum(hidden * hidden, axis=1, keepdims=True)
    scale = lax.rsqrt(square / depth + epsilon)
    for j in range(seqs):
        block = pl.ds(j * cols, cols)
        tok[r, aligned(s, rows), block] = (hid[:, block] * scale * gain[:, block]).astype(
            jnp.bfloat16
        )

    def piece(seq, role):
        return tok.at[role, aligned(seq, rows), :]

    def tz(off):
        return remote(piece(s, r), piece(s, r), tz_s.at[off], tz_r.at[off], to_role(off))

    def tz_in(off, role):
        return remote(piece(s, role), piece(s, role), tz_s.at[off], tz_r.at[off], to_role(off))

    def tx(i, seq, role):
        return remote(
            piece(seq, role), piece(seq, role), tx_s.at[i], tx_r.at[i], {"seq": side}
        )

    def tc(i, path, seq, role):
        return remote(
            piece(seq, role), piece(seq, role), tc_s.at[i, path], tc_r.at[i, path], {"seq": mate}
        )

    def yc(i, path, role):
        seq = far if path else mate
        return remote(
            y.at[role, aligned(seq, rows), :],
            y_core.at[i, path],
            yc_s.at[i, path],
            yc_r.at[i, path],
            {"seq": mate},
        )

    def yx(i, role):
        return remote(
            y.at[role, aligned(side, rows), :], y_x.at[i], yx_s.at[i], yx_r.at[i], {"seq": side}
        )

    def yz(off, role):
        return remote(
            y.at[role, aligned(s, rows), :],
            y_role.at[off],
            yz_s.at[off],
            yz_r.at[off],
            {"role": role},
        )

    tx(0, s, r).start()
    for off in offs:
        tz(off).start()
    tc(0, 0, s, r).start()
    for copy in loads[6:]:
        copy.wait()

    expert = s * roles + r
    hidden_width = act.shape[1]
    step_f = hidden_width // 3 if hidden_width % 3 == 0 else hidden_width
    gate_lane = lax.broadcasted_iota(jnp.int32, (full, LANES), 1) % (LANES // 2)

    def off_of(i):
        return (2 * i) % 3 + 3 * (i // 3)

    def role_of(i):
        return (r + roles - off_of(i)) % roles

    def pass_core(i):
        role = role_of(i)
        yc(i, 0, role).wait_recv()
        yc(i, 1, role).wait_recv()
        spot = aligned(side, rows)
        y[role, spot, :] = (
            y[role, spot, :].astype(jnp.float32) + y_core[i, 1].astype(jnp.float32)
        ).astype(jnp.bfloat16)
        yx(i, role).start()

    def summed(i):
        role = role_of(i)
        yx(i, role).wait_recv()
        return (
            y[role, aligned(s, rows), :].astype(jnp.float32)
            + y_core[i, 0].astype(jnp.float32)
            + y_x[i].astype(jnp.float32)
        )

    def pass_role(i):
        role = role_of(i)
        y[role, aligned(s, rows), :] = summed(i).astype(jnp.bfloat16)
        yz(off_of(i), role).start()

    def one_block(i, carry):
        role = role_of(i)

        @pl.when(i > 0)
        def _():
            tz_in(off_of(i), role).wait_recv()
            tx(i, s, role).start()
            tc(i, 0, s, role).start()

        tx(i, side, role).wait_recv()
        tc(i, 1, side, role).start()
        tc(i, 0, mate, role).wait_recv()
        tc(i, 1, far, role).wait_recv()

        shares = tok[role, :, depth : depth + LANES].astype(jnp.float32)
        share = jnp.sum(jnp.where(gate_lane == expert, shares, 0.0), axis=1, keepdims=True)
        inputs = tok[role, :, 0:depth]
        for start in range(0, hidden_width, step_f):
            block = pl.ds(start, step_f)
            gate = jnp.dot(inputs, gw[0, :, block], preferred_element_type=jnp.float32)
            up = jnp.dot(inputs, uw[0, :, block], preferred_element_type=jnp.float32)
            act[:, block] = (gate / (1.0 + jnp.exp(-gate)) * up).astype(jnp.bfloat16)
        for j in range(seqs):
            block = pl.ds(j * cols, cols)
            product = jnp.dot(act[...], dw[0, :, block], preferred_element_type=jnp.float32)
            y[role, :, block] = (product * share).astype(jnp.bfloat16)
        yc(i, 1, role).start()
        yc(i, 0, role).start()

        @pl.when(i > 0)
        def _():
            pass_core(i - 1)

        @pl.when(i > 2)
        def _():
            pass_role(i - 2)

        return carry

    lax.fori_loop(0, roles, one_block, 0)
    pass_core(roles - 1)
    pass_role(roles - 2)
    pass_role(roles - 1)
    total = hid[...] + summed(0)
    for off in offs:
        yz(off, r).wait_recv()
        total = total + y_role[off].astype(jnp.float32)
    out_ref[0] = total.astype(out_ref.dtype)

    for off in offs:
        for t in range(2):
            kv1(t, off).wait_send()
        for j in range(seqs):
            pr(j, off).wait_send()
        tz(off).wait_send()
        yz(off, r).wait_send()
    for path in range(3):
        for t in range(2):
            kv2(t, path, s, mate).wait_send()
        wo2(path, s, mate).wait_send()
    for i in range(roles):
        tx(i, s, r).wait_send()
        yx(i, r).wait_send()
        for path in range(2):
            tc(i, path, s, r).wait_send()
            yc(i, path, r).wait_send()


def fused(
    query_rows,
    encoded_key_rows,
    value_matrix_rows,
    output_weight,
    residual,
    norm_gain,
    route_experts,
    route_gates,
    gate_weight,
    up_weight,
    down_weight,
):
    seqs, roles = lax.axis_size("seq"), lax.axis_size("role")
    batch, rows, width = query_rows.shape
    depth, cols = residual.shape[2], output_weight.shape[1]
    hidden_width = gate_weight.shape[2]
    full = rows * seqs
    bf16, f32 = jnp.bfloat16, jnp.float32
    gain = norm_gain.reshape(1, depth)
    vmem = [
        pltpu.VMEM(query_rows.shape, bf16),
        pltpu.VMEM((2, batch, full, HEAD_WIDTH), bf16),
        pltpu.VMEM((seqs, width, cols), bf16),
        pltpu.VMEM(residual.shape, bf16),
        pltpu.VMEM(gain.shape, f32),
        pltpu.VMEM(route_experts.shape, jnp.int32),
        pltpu.VMEM(route_gates.shape, f32),
        pltpu.VMEM(gate_weight.shape, bf16),
        pltpu.VMEM(up_weight.shape, bf16),
        pltpu.VMEM(down_weight.shape, bf16),
        pltpu.VMEM((batch * rows, width), bf16),
        pltpu.VMEM((seqs, batch * rows, cols), bf16),
        pltpu.VMEM((seqs, roles, rows, cols), bf16),
        pltpu.VMEM((rows, depth), f32),
        pltpu.VMEM((roles, full, depth + LANES), bf16),
        pltpu.VMEM((full, hidden_width), bf16),
        pltpu.VMEM((roles, full, depth), bf16),
        pltpu.VMEM((roles, 2, rows, depth), bf16),
        pltpu.VMEM((roles, rows, depth), bf16),
        pltpu.VMEM((roles, rows, depth), bf16),
    ]
    dma = pltpu.SemaphoreType.DMA
    counts = [(2, roles)] * 2 + [(2, 3)] * 2 + [(3,)] * 2 + [(seqs, roles)] * 2
    counts += [(roles,)] * 4 + [(roles, 2)] * 4 + [(roles,)] * 4
    return pl.pallas_call(
        partial(layer_kernel, roles, seqs),
        out_shape=jax.ShapeDtypeStruct(residual.shape, bf16),
        in_specs=[pl.BlockSpec(memory_space=pl.ANY)] * 11,
        out_specs=pl.BlockSpec(memory_space=pltpu.VMEM),
        scratch_shapes=vmem + [dma((9,)), dma((2,))] + [dma(count) for count in counts],
        compiler_params=pltpu.CompilerParams(
            collective_id=0, has_side_effects=True, vmem_limit_bytes=60 * 1024 * 1024
        ),
    )(
        query_rows,
        encoded_key_rows,
        value_matrix_rows,
        output_weight,
        residual,
        gain,
        route_experts,
        route_gates,
        gate_weight,
        up_weight,
        down_weight,
    )


def solution(mesh):
    square = mesh.shape["seq"] == 4 and mesh.shape["role"] == KEY_VALUE_HEADS
    body = fused if square else shards
    placed = (
        P("groups", "seq", "role"),
        P("groups", ("seq", "role"), None),
        P("groups", ("seq", "role"), None),
        P("role", "seq"),
        P(("groups", "role"), "seq", None),
        P(),
        P(("groups", "role"), "seq", None),
        P(("groups", "role"), "seq", None),
        P(("seq", "role"), None, None),
        P(("seq", "role"), None, None),
        P(("seq", "role"), None, None),
    )
    return jax.shard_map(
        body,
        mesh=mesh,
        in_specs=placed,
        out_specs=P(("groups", "role"), "seq", None),
        check_vma=False,
    )
```

```python
from functools import partial

import jax
import jax.numpy as jnp
from jax import lax
from jax.experimental import pallas as pl
from jax.experimental.pallas import tpu as pltpu
from jax.sharding import PartitionSpec as P

D = 2048
QUERY_HEADS = 32
KEY_VALUE_HEADS = 4
HEAD_WIDTH = 128
TOPK = 8


epsilon = 1e-06
masked_score = -1e30


def score_block(queries, every_key, query_position, block_start, block_width, score_scale):
    keys_part = lax.slice_in_dim(every_key, block_start, block_start + block_width, axis=0)
    raw_scores = (
        jnp.einsum("qhd,kd->hqk", queries, keys_part, preferred_element_type=jnp.float32)
        * score_scale
    )
    key_position = block_start + jnp.arange(block_width, dtype=jnp.int32)
    return jnp.where(
        key_position[None, None, :] <= query_position[None, :, None], raw_scores, masked_score
    )


def value_block(rounded, every_value, block_start, block_width):
    prob_block = lax.slice_in_dim(rounded, block_start, block_start + block_width, axis=2)
    values_part = lax.slice_in_dim(every_value, block_start, block_start + block_width, axis=0)
    return jnp.einsum("hqk,kd->qhd", prob_block, values_part, preferred_element_type=jnp.float32)


def shards(
    query_rows,
    encoded_key_rows,
    value_matrix_rows,
    output_weight,
    residual,
    norm_gain,
    route_experts,
    route_gates,
    gate_weight,
    up_weight,
    down_weight,
):
    seq_count = lax.axis_size("seq")
    role_count = lax.axis_size("role")
    seq_index = lax.axis_index("seq")
    role_index = lax.axis_index("role")
    batch_count = query_rows.shape[0]
    local_length = query_rows.shape[1]
    local_heads = query_rows.shape[2] // HEAD_WIDTH
    full_length = local_length * seq_count
    query_group_width = QUERY_HEADS // KEY_VALUE_HEADS
    head_pick = role_index * local_heads // query_group_width
    role_keys, role_values = (
        lax.all_gather(encoded_key_rows, "role", axis=1, tiled=True),
        lax.all_gather(value_matrix_rows, "role", axis=1, tiled=True),
    )
    head_keys = lax.dynamic_slice_in_dim(role_keys, head_pick * HEAD_WIDTH, HEAD_WIDTH, 2)
    head_values = lax.dynamic_slice_in_dim(role_values, head_pick * HEAD_WIDTH, HEAD_WIDTH, 2)
    whole_keys, whole_values, whole_proj = (
        lax.all_gather(head_keys, "seq", axis=1, tiled=True),
        lax.all_gather(head_values, "seq", axis=1, tiled=True),
        lax.all_gather(output_weight, "seq", axis=1, tiled=True),
    )
    key_width = full_length // 8
    score_scale = HEAD_WIDTH ** (-0.5)
    query_position = seq_index * local_length + jnp.arange(local_length, dtype=jnp.int32)
    last_needed = (seq_index + 1) * local_length

    def one_sequence(operands):
        own_queries, every_key, every_value = operands
        queries = own_queries.reshape(local_length, local_heads, HEAD_WIDTH)
        pieces = []
        for number in range(8):
            block_start = number * key_width
            compute = partial(
                score_block, queries, every_key, query_position, block_start, key_width, score_scale
            )
            skipped = partial(
                jnp.full, (local_heads, local_length, key_width), masked_score, jnp.float32
            )
            pieces.append(lax.cond(block_start < last_needed, compute, skipped))
        scores = jnp.concatenate(pieces, axis=2)
        row_peak = jnp.max(scores, axis=2, keepdims=True)
        weights = jnp.exp(scores - row_peak)
        totals = jnp.sum(weights, axis=2, keepdims=True)
        rounded = weights.astype(jnp.bfloat16)
        mixed_rows = jnp.zeros((local_length, local_heads, HEAD_WIDTH), jnp.float32)
        for number in range(8):
            block_start = number * key_width
            product = partial(value_block, rounded, every_value, block_start, key_width)
            nothing = partial(jnp.zeros, (local_length, local_heads, HEAD_WIDTH), jnp.float32)
            mixed_rows = mixed_rows + lax.cond(block_start < last_needed, product, nothing)
        attended = (mixed_rows / totals.transpose(1, 0, 2)).astype(jnp.bfloat16)
        return attended.reshape(local_length, local_heads * HEAD_WIDTH)

    attended = lax.map(one_sequence, (query_rows, whole_keys, whole_values))
    flat_attended = attended.reshape(batch_count * local_length, local_heads * HEAD_WIDTH)
    projected = lax.psum_scatter(
        jnp.dot(flat_attended, whole_proj, preferred_element_type=jnp.float32).astype(jnp.bfloat16),
        "role",
        scatter_dimension=0,
        tiled=True,
    ).astype(jnp.float32)
    hidden = residual[0].astype(jnp.float32) + projected
    variance = jnp.mean(hidden * hidden, axis=-1, keepdims=True)
    normed = (hidden * lax.rsqrt(variance + epsilon) * norm_gain).astype(jnp.bfloat16)
    expert_ids = route_experts.reshape(-1)
    gate_values = route_gates.reshape(-1)
    experts_local = gate_weight.shape[0]
    device_count = seq_count * role_count
    expert_count = experts_local * device_count
    assign = expert_ids.shape[0]
    capacity = assign // expert_count + 1
    onehot = (expert_ids[:, None] == jnp.arange(expert_count, dtype=jnp.int32)[None, :]).astype(
        jnp.int32
    )
    earlier = jnp.cumsum(onehot, axis=0) - onehot
    slot_rank = jnp.sum(earlier * onehot, axis=1)
    slot_index = expert_ids * capacity + slot_rank
    source_token = jnp.arange(assign, dtype=jnp.int32) // TOPK
    slot_token = jnp.zeros((expert_count * capacity,), jnp.int32).at[slot_index].set(source_token)
    slot_used = jnp.zeros((expert_count * capacity,), jnp.bfloat16).at[slot_index].set(1.0)
    outgoing = (normed[slot_token] * slot_used[:, None]).reshape(
        device_count, experts_local, capacity, D
    )
    incoming = lax.all_to_all(outgoing, ("seq", "role"), split_axis=0, concat_axis=0, tiled=True)
    gate_hidden = jnp.einsum(
        "sjcd,jdf->sjcf", incoming, gate_weight, preferred_element_type=jnp.float32
    )
    up_hidden = jnp.einsum(
        "sjcd,jdf->sjcf", incoming, up_weight, preferred_element_type=jnp.float32
    )
    activated = (jax.nn.silu(gate_hidden) * up_hidden).astype(jnp.bfloat16)
    returned = lax.all_to_all(
        jnp.einsum(
            "sjcf,jfd->sjcd", activated, down_weight, preferred_element_type=jnp.float32
        ).astype(jnp.bfloat16),
        ("seq", "role"),
        split_axis=0,
        concat_axis=0,
        tiled=True,
    )
    gathered = returned.reshape(expert_count * capacity, D)[slot_index]
    weighted = gathered.astype(jnp.float32) * gate_values[:, None]
    expert_sum = jnp.sum(weighted.reshape(-1, TOPK, D), axis=1)
    return (hidden + expert_sum).astype(jnp.bfloat16).reshape(residual.shape)


MESH = pl.DeviceIdType.MESH
LANES = 128


def aligned(index, size):
    return pl.ds(pl.multiple_of(index * size, size), size)


def layer_kernel(
    roles,
    seqs,
    q_hbm,
    k_hbm,
    v_hbm,
    wo_hbm,
    res_hbm,
    gain_hbm,
    ids_hbm,
    gates_hbm,
    gw_hbm,
    uw_hbm,
    dw_hbm,
    out_ref,
    q,
    kv,
    wo,
    res,
    gain,
    ids,
    gates,
    gw,
    uw,
    dw,
    att,
    part,
    part_in,
    hid,
    tok,
    act,
    y,
    y_core,
    y_x,
    y_role,
    load_sem,
    own_sem,
    kv1_s,
    kv1_r,
    kv2_s,
    kv2_r,
    wm_s,
    wm_r,
    wx_s,
    wx_r,
    wy_s,
    wy_r,
    pr_s,
    pr_r,
    tz_s,
    tz_r,
    tx_s,
    tx_r,
    tc_s,
    tc_r,
    yc_s,
    yc_r,
    yx_s,
    yx_r,
    yz_s,
    yz_r,
):
    s = lax.axis_index("seq")
    r = lax.axis_index("role")
    g = lax.axis_index("groups")
    mate = s + 1 - 2 * (s % 2)
    side = (s + 2) % 4
    far = mate + 2 - 4 * (mate // 2)
    batch, rows, width = q.shape
    heads = width // HEAD_WIDTH
    own_keys = k_hbm.shape[1]
    full = rows * seqs
    cols = wo.shape[2]
    offs = (1, 2, 3)
    chunks = 4
    chunk_rows = width // (2 * chunks)

    def role_of(i):
        return (r // 2 + i // 2) % 2 * 2 + (r + i) % 2

    def remote(src, dst, ssem, rsem, device):
        return pltpu.make_async_remote_copy(
            src_ref=src,
            dst_ref=dst,
            send_sem=ssem,
            recv_sem=rsem,
            device_id=device,
            device_id_type=MESH,
        )

    def to_role(off):
        return {"role": role_of(off)}

    barrier = pltpu.get_barrier_semaphore()
    for off in offs:
        pl.semaphore_signal(barrier, inc=1, device_id=to_role(off), device_id_type=MESH)
    for peer in ({"seq": mate}, {"seq": side}, {"groups": 1 - g}):
        pl.semaphore_signal(barrier, inc=1, device_id=peer, device_id_type=MESH)

    loads = [
        pltpu.make_async_copy(a, b, load_sem.at[i])
        for i, (a, b) in enumerate(
            (
                (q_hbm, q),
                (res_hbm, res),
                (gain_hbm, gain),
                (ids_hbm, ids),
                (gates_hbm, gates),
                (wo_hbm, wo.at[s]),
                (gw_hbm, gw),
                (uw_hbm, uw),
                (dw_hbm, dw),
            )
        )
    ]
    pair = (k_hbm, v_hbm)

    def kv_spot(t, seq, role):
        return kv.at[t, :, aligned(seq * roles + role, own_keys), :]

    owns = [
        pltpu.make_async_copy(
            pair[t].at[:, :, aligned(r, HEAD_WIDTH)], kv_spot(t, s, r), own_sem.at[t]
        )
        for t in range(2)
    ]
    for copy in owns + loads[:6]:
        copy.start()
    pl.semaphore_wait(barrier, roles - 1 + 3)

    def kv1(t, off):
        return remote(
            pair[t].at[:, :, aligned(role_of(off), HEAD_WIDTH)],
            kv_spot(t, s, r),
            kv1_s.at[t, off],
            kv1_r.at[t, off],
            to_role(off),
        )

    def kv1_in(t, off):
        source = role_of(off)
        return remote(
            pair[t].at[:, :, aligned(r, HEAD_WIDTH)],
            kv_spot(t, s, source),
            kv1_s.at[t, off],
            kv1_r.at[t, off],
            to_role(off),
        )

    for off in offs:
        for t in range(2):
            kv1(t, off).start()
    for copy in loads[6:]:
        copy.start()

    def kv2(t, path, seq, target):
        spot = kv.at[t, :, aligned(seq, rows), :]
        return remote(spot, spot, kv2_s.at[t, path], kv2_r.at[t, path], {"seq": target})

    def wo_part(seq, n):
        return wo.at[seq, aligned(n, chunk_rows), :]

    def wo_own(seq):
        return remote(wo.at[seq], wo.at[seq], wm_s.at[0], wm_r.at[0], {"seq": mate})

    def wo_x(seq, c):
        spot = wo_part(seq, g * chunks + c)
        return remote(spot, spot, wx_s.at[c], wx_r.at[c], {"seq": side})

    def wo_y(half, c):
        spot = wo_part(side, half * chunks + c)
        return remote(spot, spot, wy_s.at[c], wy_r.at[c], {"groups": 1 - g})

    def wo_mate(seq, half, c, path):
        spot = wo_part(seq, half * chunks + c)
        sem = 1 + path * chunks + c
        return remote(spot, spot, wm_s.at[sem], wm_r.at[sem], {"seq": mate})

    def wo_pass(c):
        wo_x(side, c).wait_recv()
        wo_y(g, c).start()
        wo_mate(side, g, c, 0).start()

    loads[5].wait()
    wo_x(s, 0).start()
    wo_own(s).start()
    for copy in owns:
        copy.wait()
    for off in offs:
        for t in range(2):
            kv1_in(t, off).wait_recv()
    for t in range(2):
        kv2(t, 1, s, side).start()
        kv2(t, 0, s, mate).start()
    for c in range(1, chunks):
        wo_x(s, c).start()

    for copy in loads[:5]:
        copy.wait()
    lane = lax.broadcasted_iota(jnp.int32, (rows, LANES), 1)
    table = jnp.zeros((rows, LANES), jnp.float32)
    for k in range(ids.shape[2]):
        chosen = lane % (LANES // 2) == ids[0, :, k : k + 1]
        table = table + jnp.where(chosen, gates[0, :, k : k + 1], 0.0)
    high = table.astype(jnp.bfloat16)
    low = (table - high.astype(jnp.float32)).astype(jnp.bfloat16)
    depth = hid.shape[1]
    tok[r, aligned(s, rows), depth : depth + LANES] = jnp.where(
        lane < LANES // 2, high.astype(jnp.float32), low.astype(jnp.float32)
    ).astype(jnp.bfloat16)

    for t in range(2):
        kv2(t, 1, side, side).wait_recv()
        kv2(t, 2, side, mate).start()
    for t in range(2):
        kv2(t, 0, mate, mate).wait_recv()
        kv2(t, 2, far, mate).wait_recv()

    wo_pass(0)
    query_row = s * rows + lax.broadcasted_iota(jnp.int32, (rows, full), 0)
    allowed = lax.broadcasted_iota(jnp.int32, (rows, full), 1) <= query_row

    def attend(b, carry):
        keys, values = kv[0, b], kv[1, b]
        for h in range(heads):
            head = pl.ds(h * HEAD_WIDTH, HEAD_WIDTH)
            scores = lax.dot_general(
                q[b, :, head],
                keys,
                (((1,), (1,)), ((), ())),
                preferred_element_type=jnp.float32,
            ) * (HEAD_WIDTH**-0.5)
            scores = jnp.where(allowed, scores, masked_score)
            weights = jnp.exp(scores - jnp.max(scores, axis=1, keepdims=True))
            totals = jnp.sum(weights, axis=1, keepdims=True)
            mixed = jnp.dot(
                weights.astype(jnp.bfloat16), values, preferred_element_type=jnp.float32
            )
            att[aligned(b, rows), head] = (mixed / totals).astype(jnp.bfloat16)

        @pl.when(b == batch // 2)
        def _():
            wo_pass(1)

        return carry

    lax.fori_loop(0, batch, attend, 0)

    def pr(j, kind):
        return remote(
            part.at[j, aligned(role_of((1, 3, 2)[kind]), rows), :],
            part_in.at[j, kind],
            pr_s.at[j, kind],
            pr_r.at[j, kind],
            to_role((1, 1, 2)[kind]),
        )

    def project(j):
        part[j] = jnp.dot(att[...], wo[j], preferred_element_type=jnp.float32).astype(
            jnp.bfloat16
        )
        pr(j, 1).start()
        pr(j, 0).start()

    def pass_pair(j):
        pr(j, 1).wait_recv()
        spot = aligned(role_of(2), rows)
        part[j, spot, :] = (
            part[j, spot, :].astype(jnp.float32) + part_in[j, 1].astype(jnp.float32)
        ).astype(jnp.bfloat16)
        pr(j, 2).start()

    project(s)
    wo_pass(2)
    wo_own(mate).wait_recv()
    project(mate)
    wo_pass(3)
    pass_pair(s)
    pass_pair(mate)
    for c in range(chunks):
        wo_y(1 - g, c).wait_recv()
        wo_mate(side, 1 - g, c, 1).start()
    project(side)
    for c in range(chunks):
        wo_mate(far, g, c, 0).wait_recv()
        wo_mate(far, 1 - g, c, 1).wait_recv()
    project(far)
    pass_pair(side)
    pass_pair(far)

    square = jnp.zeros((rows, 1), jnp.float32)
    for j in range(seqs):
        block = pl.ds(j * cols, cols)
        total = part[j, aligned(r, rows), :].astype(jnp.float32)
        for kind in (0, 2):
            pr(j, kind).wait_recv()
            total = total + part_in[j, kind].astype(jnp.float32)
        hidden = res[0, :, block].astype(jnp.float32) + total
        hid[:, block] = hidden
        square = square + jnp.sum(hidden * hidden, axis=1, keepdims=True)
    scale = lax.rsqrt(square / depth + epsilon)
    for j in range(seqs):
        block = pl.ds(j * cols, cols)
        tok[r, aligned(s, rows), block] = (hid[:, block] * scale * gain[:, block]).astype(
            jnp.bfloat16
        )

    def piece(seq, role):
        return tok.at[role, aligned(seq, rows), :]

    def tz(kind, role, to):
        return remote(
            piece(s, role), piece(s, role), tz_s.at[kind], tz_r.at[kind], {"role": to}
        )

    def tx(i, seq, role):
        return remote(
            piece(seq, role), piece(seq, role), tx_s.at[i], tx_r.at[i], {"seq": side}
        )

    def tc(i, path, seq, role):
        return remote(
            piece(seq, role), piece(seq, role), tc_s.at[i, path], tc_r.at[i, path], {"seq": mate}
        )

    def yc(i, path, role):
        seq = far if path else mate
        return remote(
            y.at[role, aligned(seq, rows), :],
            y_core.at[i, path],
            yc_s.at[i, path],
            yc_r.at[i, path],
            {"seq": mate},
        )

    def yx(i, role):
        return remote(
            y.at[role, aligned(side, rows), :], y_x.at[i], yx_s.at[i], yx_r.at[i], {"seq": side}
        )

    def yz(kind):
        return remote(
            y.at[role_of((1, 3, 2)[kind]), aligned(s, rows), :],
            y_role.at[kind],
            yz_s.at[kind],
            yz_r.at[kind],
            to_role((1, 1, 2)[kind]),
        )

    tx(0, s, r).start()
    tz(0, r, role_of(1)).start()
    tz(1, r, role_of(2)).start()
    tc(0, 0, s, r).start()
    for copy in loads[6:]:
        copy.wait()

    expert = s * roles + r
    hidden_width = act.shape[1]
    step_f = hidden_width // 3 if hidden_width % 3 == 0 else hidden_width
    gate_lane = lax.broadcasted_iota(jnp.int32, (full, LANES), 1) % (LANES // 2)

    def pass_core(i):
        role = role_of(i)
        yc(i, 0, role).wait_recv()
        yc(i, 1, role).wait_recv()
        spot = aligned(side, rows)
        y[role, spot, :] = (
            y[role, spot, :].astype(jnp.float32) + y_core[i, 1].astype(jnp.float32)
        ).astype(jnp.bfloat16)
        yx(i, role).start()

    def summed(i):
        role = role_of(i)
        yx(i, role).wait_recv()
        return (
            y[role, aligned(s, rows), :].astype(jnp.float32)
            + y_core[i, 0].astype(jnp.float32)
            + y_x[i].astype(jnp.float32)
        )

    def settle(i, kind):
        y[role_of(i), aligned(s, rows), :] = summed(i).astype(jnp.bfloat16)
        yz(kind).start()

    def one_block(i, carry):
        role = role_of(i)

        @pl.when(i < roles - 1)
        def _():
            following = role_of(i + 1)
            tz(i, following, following).wait_recv()
            tx(i + 1, s, following).start()
            tc(i + 1, 0, s, following).start()

        @pl.when(i == 1)
        def _():
            tz(2, role_of(2), role_of(1)).start()

        tx(i, side, role).wait_recv()
        tc(i, 1, side, role).start()
        tc(i, 0, mate, role).wait_recv()
        tc(i, 1, far, role).wait_recv()

        shares = tok[role, :, depth : depth + LANES].astype(jnp.float32)
        share = jnp.sum(jnp.where(gate_lane == expert, shares, 0.0), axis=1, keepdims=True)
        inputs = tok[role, :, 0:depth]
        for start in range(0, hidden_width, step_f):
            block = pl.ds(start, step_f)
            gate = jnp.dot(inputs, gw[0, :, block], preferred_element_type=jnp.float32)
            up = jnp.dot(inputs, uw[0, :, block], preferred_element_type=jnp.float32)
            act[:, block] = (gate / (1.0 + jnp.exp(-gate)) * up).astype(jnp.bfloat16)
        for j in range(seqs):
            block = pl.ds(j * cols, cols)
            product = jnp.dot(act[...], dw[0, :, block], preferred_element_type=jnp.float32)
            y[role, :, block] = (product * share).astype(jnp.bfloat16)
        yc(i, 1, role).start()
        yc(i, 0, role).start()

        @pl.when(i > 1)
        def _():
            pass_core(i - 1)

        return carry

    lax.fori_loop(0, roles, one_block, 0)
    pass_core(3)
    pass_core(0)
    settle(1, 0)
    second = summed(2)
    settle(3, 1)
    yz(1).wait_recv()
    y[role_of(2), aligned(s, rows), :] = (second + y_role[1].astype(jnp.float32)).astype(
        jnp.bfloat16
    )
    yz(2).start()
    total = hid[...] + summed(0)
    for kind in (0, 2):
        yz(kind).wait_recv()
        total = total + y_role[kind].astype(jnp.float32)
    out_ref[0] = total.astype(out_ref.dtype)

    for off in offs:
        for t in range(2):
            kv1(t, off).wait_send()
    for kind in range(3):
        for j in range(seqs):
            pr(j, kind).wait_send()
        tz(kind, r, role_of(1)).wait_send()
        yz(kind).wait_send()
        for t in range(2):
            kv2(t, kind, s, mate).wait_send()
    wo_own(s).wait_send()
    for c in range(chunks):
        wo_x(s, c).wait_send()
        wo_y(g, c).wait_send()
        for path in range(2):
            wo_mate(s, g, c, path).wait_send()
    for i in range(roles):
        tx(i, s, r).wait_send()
        yx(i, r).wait_send()
        for path in range(2):
            tc(i, path, s, r).wait_send()
            yc(i, path, r).wait_send()


def fused(
    query_rows,
    encoded_key_rows,
    value_matrix_rows,
    output_weight,
    residual,
    norm_gain,
    route_experts,
    route_gates,
    gate_weight,
    up_weight,
    down_weight,
):
    seqs, roles = lax.axis_size("seq"), lax.axis_size("role")
    batch, rows, width = query_rows.shape
    depth, cols = residual.shape[2], output_weight.shape[1]
    hidden_width = gate_weight.shape[2]
    full = rows * seqs
    bf16, f32 = jnp.bfloat16, jnp.float32
    gain = norm_gain.reshape(1, depth)
    vmem = [
        pltpu.VMEM(query_rows.shape, bf16),
        pltpu.VMEM((2, batch, full, HEAD_WIDTH), bf16),
        pltpu.VMEM((seqs, width, cols), bf16),
        pltpu.VMEM(residual.shape, bf16),
        pltpu.VMEM(gain.shape, f32),
        pltpu.VMEM(route_experts.shape, jnp.int32),
        pltpu.VMEM(route_gates.shape, f32),
        pltpu.VMEM(gate_weight.shape, bf16),
        pltpu.VMEM(up_weight.shape, bf16),
        pltpu.VMEM(down_weight.shape, bf16),
        pltpu.VMEM((batch * rows, width), bf16),
        pltpu.VMEM((seqs, batch * rows, cols), bf16),
        pltpu.VMEM((seqs, 3, rows, cols), bf16),
        pltpu.VMEM((rows, depth), f32),
        pltpu.VMEM((roles, full, depth + LANES), bf16),
        pltpu.VMEM((full, hidden_width), bf16),
        pltpu.VMEM((roles, full, depth), bf16),
        pltpu.VMEM((roles, 2, rows, depth), bf16),
        pltpu.VMEM((roles, rows, depth), bf16),
        pltpu.VMEM((3, rows, depth), bf16),
    ]
    dma = pltpu.SemaphoreType.DMA
    counts = [(2, roles)] * 2 + [(2, 3)] * 2 + [(9,)] * 2 + [(4,)] * 4 + [(seqs, 3)] * 2
    counts += [(3,)] * 2 + [(roles,)] * 2 + [(roles, 2)] * 4 + [(roles,)] * 2 + [(3,)] * 2
    return pl.pallas_call(
        partial(layer_kernel, roles, seqs),
        out_shape=jax.ShapeDtypeStruct(residual.shape, bf16),
        in_specs=[pl.BlockSpec(memory_space=pl.ANY)] * 11,
        out_specs=pl.BlockSpec(memory_space=pltpu.VMEM),
        scratch_shapes=vmem + [dma((9,)), dma((2,))] + [dma(count) for count in counts],
        compiler_params=pltpu.CompilerParams(
            collective_id=0, has_side_effects=True, vmem_limit_bytes=60 * 1024 * 1024
        ),
    )(
        query_rows,
        encoded_key_rows,
        value_matrix_rows,
        output_weight,
        residual,
        gain,
        route_experts,
        route_gates,
        gate_weight,
        up_weight,
        down_weight,
    )


def solution(mesh):
    square = mesh.shape["seq"] == 4 and mesh.shape["role"] == 4 and mesh.shape["groups"] == 2
    body = fused if square else shards
    placed = (
        P("groups", "seq", "role"),
        P("groups", ("seq", "role"), None),
        P("groups", ("seq", "role"), None),
        P("role", "seq"),
        P(("groups", "role"), "seq", None),
        P(),
        P(("groups", "role"), "seq", None),
        P(("groups", "role"), "seq", None),
        P(("seq", "role"), None, None),
        P(("seq", "role"), None, None),
        P(("seq", "role"), None, None),
    )
    return jax.shard_map(
        body,
        mesh=mesh,
        in_specs=placed,
        out_specs=P(("groups", "role"), "seq", None),
        check_vma=False,
    )
```

```python
from functools import partial

import jax
import jax.numpy as jnp
from jax import lax
from jax.experimental import pallas as pl
from jax.experimental.pallas import tpu as pltpu
from jax.sharding import PartitionSpec as P

D = 2048
QUERY_HEADS = 32
KEY_VALUE_HEADS = 4
HEAD_WIDTH = 128
TOPK = 8


epsilon = 1e-06
masked_score = -1e30


def score_block(queries, every_key, query_position, block_start, block_width, score_scale):
    keys_part = lax.slice_in_dim(every_key, block_start, block_start + block_width, axis=0)
    raw_scores = (
        jnp.einsum("qhd,kd->hqk", queries, keys_part, preferred_element_type=jnp.float32)
        * score_scale
    )
    key_position = block_start + jnp.arange(block_width, dtype=jnp.int32)
    return jnp.where(
        key_position[None, None, :] <= query_position[None, :, None], raw_scores, masked_score
    )


def value_block(rounded, every_value, block_start, block_width):
    prob_block = lax.slice_in_dim(rounded, block_start, block_start + block_width, axis=2)
    values_part = lax.slice_in_dim(every_value, block_start, block_start + block_width, axis=0)
    return jnp.einsum("hqk,kd->qhd", prob_block, values_part, preferred_element_type=jnp.float32)


def shards(
    query_rows,
    encoded_key_rows,
    value_matrix_rows,
    output_weight,
    residual,
    norm_gain,
    route_experts,
    route_gates,
    gate_weight,
    up_weight,
    down_weight,
):
    seq_count = lax.axis_size("seq")
    role_count = lax.axis_size("role")
    seq_index = lax.axis_index("seq")
    role_index = lax.axis_index("role")
    batch_count = query_rows.shape[0]
    local_length = query_rows.shape[1]
    local_heads = query_rows.shape[2] // HEAD_WIDTH
    full_length = local_length * seq_count
    query_group_width = QUERY_HEADS // KEY_VALUE_HEADS
    head_pick = role_index * local_heads // query_group_width
    role_keys, role_values = (
        lax.all_gather(encoded_key_rows, "role", axis=1, tiled=True),
        lax.all_gather(value_matrix_rows, "role", axis=1, tiled=True),
    )
    head_keys = lax.dynamic_slice_in_dim(role_keys, head_pick * HEAD_WIDTH, HEAD_WIDTH, 2)
    head_values = lax.dynamic_slice_in_dim(role_values, head_pick * HEAD_WIDTH, HEAD_WIDTH, 2)
    whole_keys, whole_values, whole_proj = (
        lax.all_gather(head_keys, "seq", axis=1, tiled=True),
        lax.all_gather(head_values, "seq", axis=1, tiled=True),
        lax.all_gather(output_weight, "seq", axis=1, tiled=True),
    )
    key_width = full_length // 8
    score_scale = HEAD_WIDTH ** (-0.5)
    query_position = seq_index * local_length + jnp.arange(local_length, dtype=jnp.int32)
    last_needed = (seq_index + 1) * local_length

    def one_sequence(operands):
        own_queries, every_key, every_value = operands
        queries = own_queries.reshape(local_length, local_heads, HEAD_WIDTH)
        pieces = []
        for number in range(8):
            block_start = number * key_width
            compute = partial(
                score_block, queries, every_key, query_position, block_start, key_width, score_scale
            )
            skipped = partial(
                jnp.full, (local_heads, local_length, key_width), masked_score, jnp.float32
            )
            pieces.append(lax.cond(block_start < last_needed, compute, skipped))
        scores = jnp.concatenate(pieces, axis=2)
        row_peak = jnp.max(scores, axis=2, keepdims=True)
        weights = jnp.exp(scores - row_peak)
        totals = jnp.sum(weights, axis=2, keepdims=True)
        rounded = weights.astype(jnp.bfloat16)
        mixed_rows = jnp.zeros((local_length, local_heads, HEAD_WIDTH), jnp.float32)
        for number in range(8):
            block_start = number * key_width
            product = partial(value_block, rounded, every_value, block_start, key_width)
            nothing = partial(jnp.zeros, (local_length, local_heads, HEAD_WIDTH), jnp.float32)
            mixed_rows = mixed_rows + lax.cond(block_start < last_needed, product, nothing)
        attended = (mixed_rows / totals.transpose(1, 0, 2)).astype(jnp.bfloat16)
        return attended.reshape(local_length, local_heads * HEAD_WIDTH)

    attended = lax.map(one_sequence, (query_rows, whole_keys, whole_values))
    flat_attended = attended.reshape(batch_count * local_length, local_heads * HEAD_WIDTH)
    projected = lax.psum_scatter(
        jnp.dot(flat_attended, whole_proj, preferred_element_type=jnp.float32).astype(jnp.bfloat16),
        "role",
        scatter_dimension=0,
        tiled=True,
    ).astype(jnp.float32)
    hidden = residual[0].astype(jnp.float32) + projected
    variance = jnp.mean(hidden * hidden, axis=-1, keepdims=True)
    normed = (hidden * lax.rsqrt(variance + epsilon) * norm_gain).astype(jnp.bfloat16)
    expert_ids = route_experts.reshape(-1)
    gate_values = route_gates.reshape(-1)
    experts_local = gate_weight.shape[0]
    device_count = seq_count * role_count
    expert_count = experts_local * device_count
    assign = expert_ids.shape[0]
    capacity = assign // expert_count + 1
    onehot = (expert_ids[:, None] == jnp.arange(expert_count, dtype=jnp.int32)[None, :]).astype(
        jnp.int32
    )
    earlier = jnp.cumsum(onehot, axis=0) - onehot
    slot_rank = jnp.sum(earlier * onehot, axis=1)
    slot_index = expert_ids * capacity + slot_rank
    source_token = jnp.arange(assign, dtype=jnp.int32) // TOPK
    slot_token = jnp.zeros((expert_count * capacity,), jnp.int32).at[slot_index].set(source_token)
    slot_used = jnp.zeros((expert_count * capacity,), jnp.bfloat16).at[slot_index].set(1.0)
    outgoing = (normed[slot_token] * slot_used[:, None]).reshape(
        device_count, experts_local, capacity, D
    )
    incoming = lax.all_to_all(outgoing, ("seq", "role"), split_axis=0, concat_axis=0, tiled=True)
    gate_hidden = jnp.einsum(
        "sjcd,jdf->sjcf", incoming, gate_weight, preferred_element_type=jnp.float32
    )
    up_hidden = jnp.einsum(
        "sjcd,jdf->sjcf", incoming, up_weight, preferred_element_type=jnp.float32
    )
    activated = (jax.nn.silu(gate_hidden) * up_hidden).astype(jnp.bfloat16)
    returned = lax.all_to_all(
        jnp.einsum(
            "sjcf,jfd->sjcd", activated, down_weight, preferred_element_type=jnp.float32
        ).astype(jnp.bfloat16),
        ("seq", "role"),
        split_axis=0,
        concat_axis=0,
        tiled=True,
    )
    gathered = returned.reshape(expert_count * capacity, D)[slot_index]
    weighted = gathered.astype(jnp.float32) * gate_values[:, None]
    expert_sum = jnp.sum(weighted.reshape(-1, TOPK, D), axis=1)
    return (hidden + expert_sum).astype(jnp.bfloat16).reshape(residual.shape)


MESH = pl.DeviceIdType.MESH
LANES = 128


def aligned(index, size):
    return pl.ds(pl.multiple_of(index * size, size), size)


def layer_kernel(
    roles,
    seqs,
    q_hbm,
    k_hbm,
    v_hbm,
    wo_hbm,
    res_hbm,
    gain_hbm,
    ids_hbm,
    gates_hbm,
    gw_hbm,
    uw_hbm,
    dw_hbm,
    out_ref,
    q,
    kv,
    wo,
    res,
    gain,
    ids,
    gates,
    gw,
    uw,
    dw,
    att,
    part,
    part_in,
    hid,
    tok,
    act,
    y,
    y_core,
    y_x,
    y_role,
    load_sem,
    own_sem,
    kv1_s,
    kv1_r,
    kv2_s,
    kv2_r,
    wm_s,
    wm_r,
    wx_s,
    wx_r,
    wy_s,
    wy_r,
    pr_s,
    pr_r,
    tz_s,
    tz_r,
    tx_s,
    tx_r,
    tc_s,
    tc_r,
    yc_s,
    yc_r,
    yx_s,
    yx_r,
    yz_s,
    yz_r,
):
    s = lax.axis_index("seq")
    r = lax.axis_index("role")
    g = lax.axis_index("groups")
    mate = s + 1 - 2 * (s % 2)
    side = (s + 2) % 4
    far = mate + 2 - 4 * (mate // 2)
    batch, rows, width = q.shape
    heads = width // HEAD_WIDTH
    own_keys = k_hbm.shape[1]
    full = rows * seqs
    cols = wo.shape[2]
    offs = (1, 2, 3)
    chunks = 4
    chunk_rows = width // (2 * chunks)

    def role_of(i):
        return (r // 2 + i // 2) % 2 * 2 + (r + i) % 2

    def remote(src, dst, ssem, rsem, device):
        return pltpu.make_async_remote_copy(
            src_ref=src,
            dst_ref=dst,
            send_sem=ssem,
            recv_sem=rsem,
            device_id=device,
            device_id_type=MESH,
        )

    def to_role(off):
        return {"role": role_of(off)}

    barrier = pltpu.get_barrier_semaphore()
    for off in offs:
        pl.semaphore_signal(barrier, inc=1, device_id=to_role(off), device_id_type=MESH)
    for peer in ({"seq": mate}, {"seq": side}, {"groups": 1 - g}):
        pl.semaphore_signal(barrier, inc=1, device_id=peer, device_id_type=MESH)

    loads = [
        pltpu.make_async_copy(a, b, load_sem.at[i])
        for i, (a, b) in enumerate(
            (
                (q_hbm, q),
                (res_hbm, res),
                (gain_hbm, gain),
                (ids_hbm, ids),
                (gates_hbm, gates),
                (wo_hbm, wo.at[s]),
                (gw_hbm, gw),
                (uw_hbm, uw),
                (dw_hbm, dw),
            )
        )
    ]
    pair = (k_hbm, v_hbm)

    def kv_spot(t, seq, role):
        return kv.at[t, :, aligned(seq * roles + role, own_keys), :]

    owns = [
        pltpu.make_async_copy(
            pair[t].at[:, :, aligned(r, HEAD_WIDTH)], kv_spot(t, s, r), own_sem.at[t]
        )
        for t in range(2)
    ]
    for copy in owns + loads[:6]:
        copy.start()
    pl.semaphore_wait(barrier, roles - 1 + 3)

    def kv1(t, off):
        return remote(
            pair[t].at[:, :, aligned(role_of(off), HEAD_WIDTH)],
            kv_spot(t, s, r),
            kv1_s.at[t, off],
            kv1_r.at[t, off],
            to_role(off),
        )

    def kv1_in(t, off):
        source = role_of(off)
        return remote(
            pair[t].at[:, :, aligned(r, HEAD_WIDTH)],
            kv_spot(t, s, source),
            kv1_s.at[t, off],
            kv1_r.at[t, off],
            to_role(off),
        )

    for off in offs:
        for t in range(2):
            kv1(t, off).start()
    for copy in loads[6:]:
        copy.start()

    def kv2(t, path, seq, target):
        spot = kv.at[t, :, aligned(seq, rows), :]
        return remote(spot, spot, kv2_s.at[t, path], kv2_r.at[t, path], {"seq": target})

    def wo_part(seq, n):
        return wo.at[seq, aligned(n, chunk_rows), :]

    def wo_own(seq):
        return remote(wo.at[seq], wo.at[seq], wm_s.at[0], wm_r.at[0], {"seq": mate})

    def wo_x(seq, c):
        spot = wo_part(seq, g * chunks + c)
        return remote(spot, spot, wx_s.at[c], wx_r.at[c], {"seq": side})

    def wo_y(half, c):
        spot = wo_part(side, half * chunks + c)
        return remote(spot, spot, wy_s.at[c], wy_r.at[c], {"groups": 1 - g})

    def wo_mate(seq, half, c, path):
        spot = wo_part(seq, half * chunks + c)
        sem = 1 + path * chunks + c
        return remote(spot, spot, wm_s.at[sem], wm_r.at[sem], {"seq": mate})

    def wo_pass(c):
        wo_x(side, c).wait_recv()
        wo_y(g, c).start()
        wo_mate(side, g, c, 0).start()

    loads[5].wait()
    wo_x(s, 0).start()
    wo_x(s, 1).start()
    wo_own(s).start()
    for copy in owns:
        copy.wait()
    for off in offs:
        for t in range(2):
            kv1_in(t, off).wait_recv()
    for t in range(2):
        kv2(t, 1, s, side).start()
        kv2(t, 0, s, mate).start()
    for c in range(2, chunks):
        wo_x(s, c).start()

    for copy in loads[:5]:
        copy.wait()
    place = lax.broadcasted_iota(jnp.int32, (LANES, rows), 0)
    table = jnp.zeros((LANES, rows), jnp.float32)
    for k in range(ids.shape[1]):
        chosen = place % (LANES // 2) == ids[0, k : k + 1, :]
        table = table + jnp.where(chosen, gates[0, k : k + 1, :], 0.0)
    high = table.astype(jnp.bfloat16).astype(jnp.float32)
    parts = jnp.where(place < LANES // 2, high, table - high).astype(jnp.bfloat16)
    unit = (
        lax.broadcasted_iota(jnp.int32, (rows, rows), 0)
        == lax.broadcasted_iota(jnp.int32, (rows, rows), 1)
    )
    depth = hid.shape[1]
    tok[r, aligned(s, rows), depth : depth + LANES] = lax.dot_general(
        jnp.where(unit, 1.0, 0.0).astype(jnp.bfloat16),
        parts,
        (((1,), (1,)), ((), ())),
        preferred_element_type=jnp.float32,
    ).astype(jnp.bfloat16)

    for t in range(2):
        kv2(t, 1, side, side).wait_recv()
        kv2(t, 2, side, mate).start()
    for t in range(2):
        kv2(t, 0, mate, mate).wait_recv()
        kv2(t, 2, far, mate).wait_recv()

    wo_pass(0)
    wo_pass(1)
    query_row = s * rows + lax.broadcasted_iota(jnp.int32, (rows, full), 0)
    allowed = lax.broadcasted_iota(jnp.int32, (rows, full), 1) <= query_row

    def attend(b, carry):
        keys, values = kv[0, b], kv[1, b]
        for h in range(heads):
            head = pl.ds(h * HEAD_WIDTH, HEAD_WIDTH)
            scores = lax.dot_general(
                q[b, :, head],
                keys,
                (((1,), (1,)), ((), ())),
                preferred_element_type=jnp.float32,
            ) * (HEAD_WIDTH**-0.5)
            scores = jnp.where(allowed, scores, masked_score)
            weights = jnp.exp(scores - jnp.max(scores, axis=1, keepdims=True))
            totals = jnp.sum(weights, axis=1, keepdims=True)
            mixed = jnp.dot(
                weights.astype(jnp.bfloat16), values, preferred_element_type=jnp.float32
            )
            att[aligned(b, rows), head] = (mixed / totals).astype(jnp.bfloat16)

        @pl.when(b == batch // 2)
        def _():
            wo_pass(2)

        return carry

    lax.fori_loop(0, batch, attend, 0)

    def pr(j, kind):
        return remote(
            part.at[j, aligned(role_of((1, 3, 2)[kind]), rows), :],
            part_in.at[j, kind],
            pr_s.at[j, kind],
            pr_r.at[j, kind],
            to_role((1, 1, 2)[kind]),
        )

    def project(j):
        part[j] = jnp.dot(att[...], wo[j], preferred_element_type=jnp.float32).astype(
            jnp.bfloat16
        )
        pr(j, 1).start()
        pr(j, 0).start()

    def pass_pair(j):
        pr(j, 1).wait_recv()
        spot = aligned(role_of(2), rows)
        part[j, spot, :] = (
            part[j, spot, :].astype(jnp.float32) + part_in[j, 1].astype(jnp.float32)
        ).astype(jnp.bfloat16)
        pr(j, 2).start()

    wo_pass(3)
    project(s)
    wo_own(mate).wait_recv()
    project(mate)
    pass_pair(s)
    pass_pair(mate)
    for c in range(chunks):
        wo_y(1 - g, c).wait_recv()
        wo_mate(side, 1 - g, c, 1).start()
    project(side)
    for c in range(chunks):
        wo_mate(far, g, c, 0).wait_recv()
        wo_mate(far, 1 - g, c, 1).wait_recv()
    project(far)
    pass_pair(side)
    pass_pair(far)

    square = jnp.zeros((rows, 1), jnp.float32)
    for j in range(seqs):
        block = pl.ds(j * cols, cols)
        total = part[j, aligned(r, rows), :].astype(jnp.float32)
        for kind in (0, 2):
            pr(j, kind).wait_recv()
            total = total + part_in[j, kind].astype(jnp.float32)
        hidden = res[0, :, block].astype(jnp.float32) + total
        hid[:, block] = hidden
        square = square + jnp.sum(hidden * hidden, axis=1, keepdims=True)
    scale = lax.rsqrt(square / depth + epsilon)
    for j in range(seqs):
        block = pl.ds(j * cols, cols)
        tok[r, aligned(s, rows), block] = (hid[:, block] * scale * gain[:, block]).astype(
            jnp.bfloat16
        )

    def piece(seq, role):
        return tok.at[role, aligned(seq, rows), :]

    def tz(kind, role, to):
        return remote(
            piece(s, role), piece(s, role), tz_s.at[kind], tz_r.at[kind], {"role": to}
        )

    def tx(i, seq, role):
        return remote(
            piece(seq, role), piece(seq, role), tx_s.at[i], tx_r.at[i], {"seq": side}
        )

    def tc(i, path, seq, role):
        return remote(
            piece(seq, role), piece(seq, role), tc_s.at[i, path], tc_r.at[i, path], {"seq": mate}
        )

    half = depth // 2

    def yc(i, path, role, h):
        seq = far if path else mate
        block = pl.ds(h * half, half)
        return remote(
            y.at[role, aligned(seq, rows), block],
            y_core.at[i, path, :, block],
            yc_s.at[i, path * 2 + h],
            yc_r.at[i, path * 2 + h],
            {"seq": mate},
        )

    def yx(i, role, h):
        block = pl.ds(h * half, half)
        return remote(
            y.at[role, aligned(side, rows), block],
            y_x.at[i, :, block],
            yx_s.at[i, h],
            yx_r.at[i, h],
            {"seq": side},
        )

    def yz(kind, h):
        block = pl.ds(h * half, half)
        return remote(
            y.at[role_of((1, 3, 2)[kind]), aligned(s, rows), block],
            y_role.at[kind, :, block],
            yz_s.at[kind, h],
            yz_r.at[kind, h],
            to_role((1, 1, 2)[kind]),
        )

    tx(0, s, r).start()
    tz(0, r, role_of(1)).start()
    tz(1, r, role_of(2)).start()
    tc(0, 0, s, r).start()
    for copy in loads[6:]:
        copy.wait()

    expert = s * roles + r
    hidden_width = act.shape[1]
    step_f = hidden_width // 3 if hidden_width % 3 == 0 else hidden_width
    gate_lane = lax.broadcasted_iota(jnp.int32, (full, LANES), 1) % (LANES // 2)

    def pass_core(i, h):
        role = role_of(i)
        block = pl.ds(h * half, half)
        yc(i, 1, role, h).wait_recv()
        spot = aligned(side, rows)
        y[role, spot, block] = (
            y[role, spot, block].astype(jnp.float32) + y_core[i, 1, :, block].astype(jnp.float32)
        ).astype(jnp.bfloat16)
        yx(i, role, h).start()

    def summed(i, h):
        role = role_of(i)
        block = pl.ds(h * half, half)
        yc(i, 0, role, h).wait_recv()
        yx(i, role, h).wait_recv()
        return (
            y[role, aligned(s, rows), block].astype(jnp.float32)
            + y_core[i, 0, :, block].astype(jnp.float32)
            + y_x[i, :, block].astype(jnp.float32)
        )

    def settle(i, kind, h):
        block = pl.ds(h * half, half)
        y[role_of(i), aligned(s, rows), block] = summed(i, h).astype(jnp.bfloat16)
        yz(kind, h).start()

    def one_block(i, carry):
        role = role_of(i)

        @pl.when(i < roles - 1)
        def _():
            following = role_of(i + 1)
            tz(i, following, following).wait_recv()
            tx(i + 1, s, following).start()
            tc(i + 1, 0, s, following).start()

        @pl.when(i == 1)
        def _():
            tz(2, role_of(2), role_of(1)).start()

        tx(i, side, role).wait_recv()
        tc(i, 1, side, role).start()
        tc(i, 0, mate, role).wait_recv()
        tc(i, 1, far, role).wait_recv()

        shares = tok[role, :, depth : depth + LANES].astype(jnp.float32)
        share = jnp.sum(jnp.where(gate_lane == expert, shares, 0.0), axis=1, keepdims=True)
        inputs = tok[role, :, 0:depth]
        for start in range(0, hidden_width, step_f):
            block = pl.ds(start, step_f)
            gate = jnp.dot(inputs, gw[0, :, block], preferred_element_type=jnp.float32)
            up = jnp.dot(inputs, uw[0, :, block], preferred_element_type=jnp.float32)
            act[:, block] = (gate / (1.0 + jnp.exp(-gate)) * up).astype(jnp.bfloat16)
        for j in range(seqs):
            block = pl.ds(j * cols, cols)
            product = jnp.dot(act[...], dw[0, :, block], preferred_element_type=jnp.float32)
            y[role, :, block] = (product * share).astype(jnp.bfloat16)
            if j % (seqs // 2) == seqs // 2 - 1:
                yc(i, 1, role, j // (seqs // 2)).start()
                yc(i, 0, role, j // (seqs // 2)).start()

        @pl.when(i > 1)
        def _():
            for h in range(2):
                pass_core(i - 1, h)

        return carry

    lax.fori_loop(0, roles, one_block, 0)
    for h in range(2):
        pass_core(3, h)
    for h in range(2):
        pass_core(0, h)
    for h in range(2):
        settle(1, 0, h)
    for h in range(2):
        settle(3, 1, h)
    for h in range(2):
        block = pl.ds(h * half, half)
        second = summed(2, h)
        yz(1, h).wait_recv()
        y[role_of(2), aligned(s, rows), block] = (
            second + y_role[1, :, block].astype(jnp.float32)
        ).astype(jnp.bfloat16)
        yz(2, h).start()
    for h in range(2):
        block = pl.ds(h * half, half)
        total = hid[:, block] + summed(0, h)
        for kind in (0, 2):
            yz(kind, h).wait_recv()
            total = total + y_role[kind, :, block].astype(jnp.float32)
        out_ref[0, :, block] = total.astype(out_ref.dtype)

    for off in offs:
        for t in range(2):
            kv1(t, off).wait_send()
    for kind in range(3):
        for j in range(seqs):
            pr(j, kind).wait_send()
        tz(kind, r, role_of(1)).wait_send()
        for h in range(2):
            yz(kind, h).wait_send()
        for t in range(2):
            kv2(t, kind, s, mate).wait_send()
    wo_own(s).wait_send()
    for c in range(chunks):
        wo_x(s, c).wait_send()
        wo_y(g, c).wait_send()
        for path in range(2):
            wo_mate(s, g, c, path).wait_send()
    for i in range(roles):
        tx(i, s, r).wait_send()
        for path in range(2):
            yx(i, r, path).wait_send()
            tc(i, path, s, r).wait_send()
            for h in range(2):
                yc(i, path, r, h).wait_send()


def fused(
    query_rows,
    encoded_key_rows,
    value_matrix_rows,
    output_weight,
    residual,
    norm_gain,
    route_experts,
    route_gates,
    gate_weight,
    up_weight,
    down_weight,
):
    seqs, roles = lax.axis_size("seq"), lax.axis_size("role")
    batch, rows, width = query_rows.shape
    depth, cols = residual.shape[2], output_weight.shape[1]
    hidden_width = gate_weight.shape[2]
    full = rows * seqs
    bf16, f32 = jnp.bfloat16, jnp.float32
    gain = norm_gain.reshape(1, depth)
    route_experts = route_experts.transpose(0, 2, 1)
    route_gates = route_gates.transpose(0, 2, 1)
    vmem = [
        pltpu.VMEM(query_rows.shape, bf16),
        pltpu.VMEM((2, batch, full, HEAD_WIDTH), bf16),
        pltpu.VMEM((seqs, width, cols), bf16),
        pltpu.VMEM(residual.shape, bf16),
        pltpu.VMEM(gain.shape, f32),
        pltpu.VMEM(route_experts.shape, jnp.int32),
        pltpu.VMEM(route_gates.shape, f32),
        pltpu.VMEM(gate_weight.shape, bf16),
        pltpu.VMEM(up_weight.shape, bf16),
        pltpu.VMEM(down_weight.shape, bf16),
        pltpu.VMEM((batch * rows, width), bf16),
        pltpu.VMEM((seqs, batch * rows, cols), bf16),
        pltpu.VMEM((seqs, 3, rows, cols), bf16),
        pltpu.VMEM((rows, depth), f32),
        pltpu.VMEM((roles, full, depth + LANES), bf16),
        pltpu.VMEM((full, hidden_width), bf16),
        pltpu.VMEM((roles, full, depth), bf16),
        pltpu.VMEM((roles, 2, rows, depth), bf16),
        pltpu.VMEM((roles, rows, depth), bf16),
        pltpu.VMEM((3, rows, depth), bf16),
    ]
    dma = pltpu.SemaphoreType.DMA
    counts = [(2, roles)] * 2 + [(2, 3)] * 2 + [(9,)] * 2 + [(4,)] * 4 + [(seqs, 3)] * 2
    counts += [(3,)] * 2 + [(roles,)] * 2 + [(roles, 2)] * 2 + [(roles, 4)] * 2
    counts += [(roles, 2)] * 2 + [(3, 2)] * 2
    return pl.pallas_call(
        partial(layer_kernel, roles, seqs),
        out_shape=jax.ShapeDtypeStruct(residual.shape, bf16),
        in_specs=[pl.BlockSpec(memory_space=pl.ANY)] * 11,
        out_specs=pl.BlockSpec(memory_space=pltpu.VMEM),
        scratch_shapes=vmem + [dma((9,)), dma((2,))] + [dma(count) for count in counts],
        compiler_params=pltpu.CompilerParams(
            collective_id=0, has_side_effects=True, vmem_limit_bytes=60 * 1024 * 1024
        ),
    )(
        query_rows,
        encoded_key_rows,
        value_matrix_rows,
        output_weight,
        residual,
        gain,
        route_experts,
        route_gates,
        gate_weight,
        up_weight,
        down_weight,
    )


def solution(mesh):
    square = mesh.shape["seq"] == 4 and mesh.shape["role"] == 4 and mesh.shape["groups"] == 2
    body = fused if square else shards
    placed = (
        P("groups", "seq", "role"),
        P("groups", ("seq", "role"), None),
        P("groups", ("seq", "role"), None),
        P("role", "seq"),
        P(("groups", "role"), "seq", None),
        P(),
        P(("groups", "role"), "seq", None),
        P(("groups", "role"), "seq", None),
        P(("seq", "role"), None, None),
        P(("seq", "role"), None, None),
        P(("seq", "role"), None, None),
    )
    return jax.shard_map(
        body,
        mesh=mesh,
        in_specs=placed,
        out_specs=P(("groups", "role"), "seq", None),
        check_vma=False,
    )
```

```python
from functools import partial

import jax
import jax.numpy as jnp
from jax import lax
from jax.experimental import pallas as pl
from jax.experimental.pallas import tpu as pltpu
from jax.sharding import PartitionSpec as P

D = 2048
QUERY_HEADS = 32
KEY_VALUE_HEADS = 4
HEAD_WIDTH = 128
TOPK = 8


epsilon = 1e-06
masked_score = -1e30


def score_block(queries, every_key, query_position, block_start, block_width, score_scale):
    keys_part = lax.slice_in_dim(every_key, block_start, block_start + block_width, axis=0)
    raw_scores = (
        jnp.einsum("qhd,kd->hqk", queries, keys_part, preferred_element_type=jnp.float32)
        * score_scale
    )
    key_position = block_start + jnp.arange(block_width, dtype=jnp.int32)
    return jnp.where(
        key_position[None, None, :] <= query_position[None, :, None], raw_scores, masked_score
    )


def value_block(rounded, every_value, block_start, block_width):
    prob_block = lax.slice_in_dim(rounded, block_start, block_start + block_width, axis=2)
    values_part = lax.slice_in_dim(every_value, block_start, block_start + block_width, axis=0)
    return jnp.einsum("hqk,kd->qhd", prob_block, values_part, preferred_element_type=jnp.float32)


def shards(
    query_rows,
    encoded_key_rows,
    value_matrix_rows,
    output_weight,
    residual,
    norm_gain,
    route_experts,
    route_gates,
    gate_weight,
    up_weight,
    down_weight,
):
    seq_count = lax.axis_size("seq")
    role_count = lax.axis_size("role")
    seq_index = lax.axis_index("seq")
    role_index = lax.axis_index("role")
    batch_count = query_rows.shape[0]
    local_length = query_rows.shape[1]
    local_heads = query_rows.shape[2] // HEAD_WIDTH
    full_length = local_length * seq_count
    query_group_width = QUERY_HEADS // KEY_VALUE_HEADS
    head_pick = role_index * local_heads // query_group_width
    role_keys, role_values = (
        lax.all_gather(encoded_key_rows, "role", axis=1, tiled=True),
        lax.all_gather(value_matrix_rows, "role", axis=1, tiled=True),
    )
    head_keys = lax.dynamic_slice_in_dim(role_keys, head_pick * HEAD_WIDTH, HEAD_WIDTH, 2)
    head_values = lax.dynamic_slice_in_dim(role_values, head_pick * HEAD_WIDTH, HEAD_WIDTH, 2)
    whole_keys, whole_values, whole_proj = (
        lax.all_gather(head_keys, "seq", axis=1, tiled=True),
        lax.all_gather(head_values, "seq", axis=1, tiled=True),
        lax.all_gather(output_weight, "seq", axis=1, tiled=True),
    )
    key_width = full_length // 8
    score_scale = HEAD_WIDTH ** (-0.5)
    query_position = seq_index * local_length + jnp.arange(local_length, dtype=jnp.int32)
    last_needed = (seq_index + 1) * local_length

    def one_sequence(operands):
        own_queries, every_key, every_value = operands
        queries = own_queries.reshape(local_length, local_heads, HEAD_WIDTH)
        pieces = []
        for number in range(8):
            block_start = number * key_width
            compute = partial(
                score_block, queries, every_key, query_position, block_start, key_width, score_scale
            )
            skipped = partial(
                jnp.full, (local_heads, local_length, key_width), masked_score, jnp.float32
            )
            pieces.append(lax.cond(block_start < last_needed, compute, skipped))
        scores = jnp.concatenate(pieces, axis=2)
        row_peak = jnp.max(scores, axis=2, keepdims=True)
        weights = jnp.exp(scores - row_peak)
        totals = jnp.sum(weights, axis=2, keepdims=True)
        rounded = weights.astype(jnp.bfloat16)
        mixed_rows = jnp.zeros((local_length, local_heads, HEAD_WIDTH), jnp.float32)
        for number in range(8):
            block_start = number * key_width
            product = partial(value_block, rounded, every_value, block_start, key_width)
            nothing = partial(jnp.zeros, (local_length, local_heads, HEAD_WIDTH), jnp.float32)
            mixed_rows = mixed_rows + lax.cond(block_start < last_needed, product, nothing)
        attended = (mixed_rows / totals.transpose(1, 0, 2)).astype(jnp.bfloat16)
        return attended.reshape(local_length, local_heads * HEAD_WIDTH)

    attended = lax.map(one_sequence, (query_rows, whole_keys, whole_values))
    flat_attended = attended.reshape(batch_count * local_length, local_heads * HEAD_WIDTH)
    projected = lax.psum_scatter(
        jnp.dot(flat_attended, whole_proj, preferred_element_type=jnp.float32).astype(jnp.bfloat16),
        "role",
        scatter_dimension=0,
        tiled=True,
    ).astype(jnp.float32)
    hidden = residual[0].astype(jnp.float32) + projected
    variance = jnp.mean(hidden * hidden, axis=-1, keepdims=True)
    normed = (hidden * lax.rsqrt(variance + epsilon) * norm_gain).astype(jnp.bfloat16)
    expert_ids = route_experts.reshape(-1)
    gate_values = route_gates.reshape(-1)
    experts_local = gate_weight.shape[0]
    device_count = seq_count * role_count
    expert_count = experts_local * device_count
    assign = expert_ids.shape[0]
    capacity = assign // expert_count + 1
    onehot = (expert_ids[:, None] == jnp.arange(expert_count, dtype=jnp.int32)[None, :]).astype(
        jnp.int32
    )
    earlier = jnp.cumsum(onehot, axis=0) - onehot
    slot_rank = jnp.sum(earlier * onehot, axis=1)
    slot_index = expert_ids * capacity + slot_rank
    source_token = jnp.arange(assign, dtype=jnp.int32) // TOPK
    slot_token = jnp.zeros((expert_count * capacity,), jnp.int32).at[slot_index].set(source_token)
    slot_used = jnp.zeros((expert_count * capacity,), jnp.bfloat16).at[slot_index].set(1.0)
    outgoing = (normed[slot_token] * slot_used[:, None]).reshape(
        device_count, experts_local, capacity, D
    )
    incoming = lax.all_to_all(outgoing, ("seq", "role"), split_axis=0, concat_axis=0, tiled=True)
    gate_hidden = jnp.einsum(
        "sjcd,jdf->sjcf", incoming, gate_weight, preferred_element_type=jnp.float32
    )
    up_hidden = jnp.einsum(
        "sjcd,jdf->sjcf", incoming, up_weight, preferred_element_type=jnp.float32
    )
    activated = (jax.nn.silu(gate_hidden) * up_hidden).astype(jnp.bfloat16)
    returned = lax.all_to_all(
        jnp.einsum(
            "sjcf,jfd->sjcd", activated, down_weight, preferred_element_type=jnp.float32
        ).astype(jnp.bfloat16),
        ("seq", "role"),
        split_axis=0,
        concat_axis=0,
        tiled=True,
    )
    gathered = returned.reshape(expert_count * capacity, D)[slot_index]
    weighted = gathered.astype(jnp.float32) * gate_values[:, None]
    expert_sum = jnp.sum(weighted.reshape(-1, TOPK, D), axis=1)
    return (hidden + expert_sum).astype(jnp.bfloat16).reshape(residual.shape)


MESH = pl.DeviceIdType.MESH
LANES = 128


def aligned(index, size):
    return pl.ds(pl.multiple_of(index * size, size), size)


def layer_kernel(
    roles,
    seqs,
    q_hbm,
    k_hbm,
    v_hbm,
    wo_hbm,
    res_hbm,
    gain_hbm,
    ids_hbm,
    gates_hbm,
    gw_hbm,
    uw_hbm,
    dw_hbm,
    out_ref,
    q,
    kv,
    wo,
    res,
    gain,
    ids,
    gates,
    gw,
    uw,
    dw,
    att,
    part,
    part_in,
    hid,
    tok,
    act,
    y,
    y_core,
    y_x,
    y_role,
    load_sem,
    own_sem,
    kv1_s,
    kv1_r,
    kv2_s,
    kv2_r,
    wm_s,
    wm_r,
    wx_s,
    wx_r,
    wy_s,
    wy_r,
    pr_s,
    pr_r,
    tz_s,
    tz_r,
    tx_s,
    tx_r,
    tc_s,
    tc_r,
    yc_s,
    yc_r,
    yx_s,
    yx_r,
    yz_s,
    yz_r,
):
    s = lax.axis_index("seq")
    r = lax.axis_index("role")
    g = lax.axis_index("groups")
    mate = s + 1 - 2 * (s % 2)
    side = (s + 2) % 4
    far = mate + 2 - 4 * (mate // 2)
    batch, rows, width = q.shape
    heads = width // HEAD_WIDTH
    own_keys = k_hbm.shape[1]
    full = rows * seqs
    cols = wo.shape[2]
    offs = (1, 2, 3)
    chunks = 4
    chunk_rows = width // (2 * chunks)

    def role_of(i):
        return (r // 2 + i // 2) % 2 * 2 + (r + i) % 2

    def remote(src, dst, ssem, rsem, device):
        return pltpu.make_async_remote_copy(
            src_ref=src,
            dst_ref=dst,
            send_sem=ssem,
            recv_sem=rsem,
            device_id=device,
            device_id_type=MESH,
        )

    def to_role(off):
        return {"role": role_of(off)}

    barrier = pltpu.get_barrier_semaphore()
    for off in offs:
        pl.semaphore_signal(barrier, inc=1, device_id=to_role(off), device_id_type=MESH)
    for peer in ({"seq": mate}, {"seq": side}, {"groups": 1 - g}):
        pl.semaphore_signal(barrier, inc=1, device_id=peer, device_id_type=MESH)

    loads = [
        pltpu.make_async_copy(a, b, load_sem.at[i])
        for i, (a, b) in enumerate(
            (
                (q_hbm, q),
                (res_hbm, res),
                (gain_hbm, gain),
                (ids_hbm, ids),
                (gates_hbm, gates),
                (wo_hbm, wo.at[s]),
                (gw_hbm, gw),
                (uw_hbm, uw),
                (dw_hbm, dw),
            )
        )
    ]
    pair = (k_hbm, v_hbm)

    def kv_spot(t, seq, role):
        return kv.at[t, :, aligned(seq * roles + role, own_keys), :]

    owns = [
        pltpu.make_async_copy(
            pair[t].at[:, :, aligned(r, HEAD_WIDTH)], kv_spot(t, s, r), own_sem.at[t]
        )
        for t in range(2)
    ]
    for copy in owns + loads[:6]:
        copy.start()
    pl.semaphore_wait(barrier, roles - 1 + 3)

    def kv1(t, off):
        return remote(
            pair[t].at[:, :, aligned(role_of(off), HEAD_WIDTH)],
            kv_spot(t, s, r),
            kv1_s.at[t, off],
            kv1_r.at[t, off],
            to_role(off),
        )

    def kv1_in(t, off):
        source = role_of(off)
        return remote(
            pair[t].at[:, :, aligned(r, HEAD_WIDTH)],
            kv_spot(t, s, source),
            kv1_s.at[t, off],
            kv1_r.at[t, off],
            to_role(off),
        )

    for off in offs:
        for t in range(2):
            kv1(t, off).start()
    for copy in loads[6:]:
        copy.start()

    def kv2(t, path, seq, target):
        spot = kv.at[t, :, aligned(seq, rows), :]
        return remote(spot, spot, kv2_s.at[t, path], kv2_r.at[t, path], {"seq": target})

    def wo_part(seq, n):
        return wo.at[seq, aligned(n, chunk_rows), :]

    def wo_own(seq):
        return remote(wo.at[seq], wo.at[seq], wm_s.at[0], wm_r.at[0], {"seq": mate})

    def wo_x(seq, c):
        spot = wo_part(seq, g * chunks + c)
        return remote(spot, spot, wx_s.at[c], wx_r.at[c], {"seq": side})

    def wo_y(half, c):
        spot = wo_part(side, half * chunks + c)
        return remote(spot, spot, wy_s.at[c], wy_r.at[c], {"groups": 1 - g})

    def wo_mate(seq, half, c, path):
        spot = wo_part(seq, half * chunks + c)
        sem = 1 + path * chunks + c
        return remote(spot, spot, wm_s.at[sem], wm_r.at[sem], {"seq": mate})

    def wo_pass(c):
        wo_x(side, c).wait_recv()
        wo_y(g, c).start()
        wo_mate(side, g, c, 0).start()

    loads[5].wait()
    wo_x(s, 0).start()
    wo_x(s, 1).start()
    wo_own(s).start()
    for copy in owns:
        copy.wait()
    for off in offs:
        for t in range(2):
            kv1_in(t, off).wait_recv()
    for t in range(2):
        kv2(t, 1, s, side).start()
        kv2(t, 0, s, mate).start()
    for c in range(2, chunks):
        wo_x(s, c).start()

    for copy in loads[:5]:
        copy.wait()
    place = lax.broadcasted_iota(jnp.int32, (LANES, rows), 0)
    table = jnp.zeros((LANES, rows), jnp.float32)
    for k in range(ids.shape[1]):
        chosen = place % (LANES // 2) == ids[0, k : k + 1, :]
        table = table + jnp.where(chosen, gates[0, k : k + 1, :], 0.0)
    high = table.astype(jnp.bfloat16).astype(jnp.float32)
    parts = jnp.where(place < LANES // 2, high, table - high).astype(jnp.bfloat16)
    unit = (
        lax.broadcasted_iota(jnp.int32, (rows, rows), 0)
        == lax.broadcasted_iota(jnp.int32, (rows, rows), 1)
    )
    depth = hid.shape[1]
    tok[r, aligned(s, rows), depth : depth + LANES] = lax.dot_general(
        jnp.where(unit, 1.0, 0.0).astype(jnp.bfloat16),
        parts,
        (((1,), (1,)), ((), ())),
        preferred_element_type=jnp.float32,
    ).astype(jnp.bfloat16)

    for t in range(2):
        kv2(t, 1, side, side).wait_recv()
        kv2(t, 2, side, mate).start()
    for t in range(2):
        kv2(t, 0, mate, mate).wait_recv()
        kv2(t, 2, far, mate).wait_recv()

    wo_pass(0)
    wo_pass(1)
    query_row = s * rows + lax.broadcasted_iota(jnp.int32, (rows, full), 0)
    allowed = lax.broadcasted_iota(jnp.int32, (rows, full), 1) <= query_row

    def attend(b, carry):
        keys, values = kv[0, b], kv[1, b]
        for h in range(heads):
            head = pl.ds(h * HEAD_WIDTH, HEAD_WIDTH)
            scores = lax.dot_general(
                q[b, :, head],
                keys,
                (((1,), (1,)), ((), ())),
                preferred_element_type=jnp.float32,
            ) * (HEAD_WIDTH**-0.5)
            scores = jnp.where(allowed, scores, masked_score)
            weights = jnp.exp(scores - jnp.max(scores, axis=1, keepdims=True))
            totals = jnp.sum(weights, axis=1, keepdims=True)
            mixed = jnp.dot(
                weights.astype(jnp.bfloat16), values, preferred_element_type=jnp.float32
            )
            att[aligned(b, rows), head] = (mixed / totals).astype(jnp.bfloat16)

        @pl.when(b == batch // 2)
        def _():
            wo_pass(2)

        return carry

    lax.fori_loop(0, batch, attend, 0)

    def pr(j, kind):
        return remote(
            part.at[j, aligned(role_of((1, 3, 2)[kind]), rows), :],
            part_in.at[j, kind],
            pr_s.at[j, kind],
            pr_r.at[j, kind],
            to_role((1, 1, 2)[kind]),
        )

    def project(j):
        part[j] = jnp.dot(att[...], wo[j], preferred_element_type=jnp.float32).astype(
            jnp.bfloat16
        )
        pr(j, 1).start()
        pr(j, 0).start()

    def pass_pair(j):
        pr(j, 1).wait_recv()
        spot = aligned(role_of(2), rows)
        part[j, spot, :] = (
            part[j, spot, :].astype(jnp.float32) + part_in[j, 1].astype(jnp.float32)
        ).astype(jnp.bfloat16)
        pr(j, 2).start()

    wo_pass(3)
    project(s)
    wo_own(mate).wait_recv()
    project(mate)
    pass_pair(s)
    pass_pair(mate)
    for c in range(chunks):
        wo_y(1 - g, c).wait_recv()
        wo_mate(side, 1 - g, c, 1).start()
    project(side)
    for c in range(chunks):
        wo_mate(far, g, c, 0).wait_recv()
        wo_mate(far, 1 - g, c, 1).wait_recv()
    project(far)
    pass_pair(side)
    pass_pair(far)

    square = jnp.zeros((rows, 1), jnp.float32)
    for j in range(seqs):
        block = pl.ds(j * cols, cols)
        total = part[j, aligned(r, rows), :].astype(jnp.float32)
        for kind in (0, 2):
            pr(j, kind).wait_recv()
            total = total + part_in[j, kind].astype(jnp.float32)
        hidden = res[0, :, block].astype(jnp.float32) + total
        hid[:, block] = hidden
        square = square + jnp.sum(hidden * hidden, axis=1, keepdims=True)
    scale = lax.rsqrt(square / depth + epsilon)
    for j in range(seqs):
        block = pl.ds(j * cols, cols)
        tok[r, aligned(s, rows), block] = (hid[:, block] * scale * gain[:, block]).astype(
            jnp.bfloat16
        )

    def piece(seq, role):
        return tok.at[role, aligned(seq, rows), :]

    def tz(kind, role, to):
        return remote(
            piece(s, role), piece(s, role), tz_s.at[kind], tz_r.at[kind], {"role": to}
        )

    def tx(i, seq, role):
        return remote(
            piece(seq, role), piece(seq, role), tx_s.at[i], tx_r.at[i], {"seq": side}
        )

    def tc(i, path, seq, role):
        return remote(
            piece(seq, role), piece(seq, role), tc_s.at[i, path], tc_r.at[i, path], {"seq": mate}
        )

    half = depth // 2

    def yc(i, path, role, h):
        seq = far if path else mate
        block = pl.ds(h * half, half)
        return remote(
            y.at[role, aligned(seq, rows), block],
            y_core.at[i, path, :, block],
            yc_s.at[i, path * 2 + h],
            yc_r.at[i, path * 2 + h],
            {"seq": mate},
        )

    def yx(i, role, h):
        block = pl.ds(h * half, half)
        return remote(
            y.at[role, aligned(side, rows), block],
            y_x.at[i, :, block],
            yx_s.at[i, h],
            yx_r.at[i, h],
            {"seq": side},
        )

    def yz(kind, h):
        block = pl.ds(h * half, half)
        return remote(
            y.at[role_of((1, 3, 2)[kind]), aligned(s, rows), block],
            y_role.at[kind, :, block],
            yz_s.at[kind, h],
            yz_r.at[kind, h],
            to_role((1, 1, 2)[kind]),
        )

    tx(0, s, r).start()
    tz(0, r, role_of(1)).start()
    tz(1, r, role_of(2)).start()
    tc(0, 0, s, r).start()
    for copy in loads[6:]:
        copy.wait()

    expert = s * roles + r
    hidden_width = act.shape[1]
    step_f = hidden_width // 3 if hidden_width % 3 == 0 else hidden_width
    gate_lane = lax.broadcasted_iota(jnp.int32, (full, LANES), 1) % (LANES // 2)

    def pass_core(i, h):
        role = role_of(i)
        block = pl.ds(h * half, half)
        yc(i, 1, role, h).wait_recv()
        spot = aligned(side, rows)
        y[role, spot, block] = (
            y[role, spot, block].astype(jnp.float32) + y_core[i, 1, :, block].astype(jnp.float32)
        ).astype(jnp.bfloat16)
        yx(i, role, h).start()

    def summed(i, h):
        role = role_of(i)
        block = pl.ds(h * half, half)
        yc(i, 0, role, h).wait_recv()
        yx(i, role, h).wait_recv()
        return (
            y[role, aligned(s, rows), block].astype(jnp.float32)
            + y_core[i, 0, :, block].astype(jnp.float32)
            + y_x[i, :, block].astype(jnp.float32)
        )

    def settle(i, kind, h):
        block = pl.ds(h * half, half)
        y[role_of(i), aligned(s, rows), block] = summed(i, h).astype(jnp.bfloat16)
        yz(kind, h).start()

    def one_block(i, carry):
        role = role_of(i)

        @pl.when(i < roles - 1)
        def _():
            following = role_of(i + 1)
            tz(i, following, following).wait_recv()
            tx(i + 1, s, following).start()
            tc(i + 1, 0, s, following).start()

        @pl.when(i == 1)
        def _():
            tz(2, role_of(2), role_of(1)).start()

        tx(i, side, role).wait_recv()
        tc(i, 1, side, role).start()
        tc(i, 0, mate, role).wait_recv()
        tc(i, 1, far, role).wait_recv()

        @pl.when(i > 1)
        def _():
            for h in range(2):
                pass_core(i - 1, h)

        shares = tok[role, :, depth : depth + LANES].astype(jnp.float32)
        share = jnp.sum(jnp.where(gate_lane == expert, shares, 0.0), axis=1, keepdims=True)
        inputs = tok[role, :, 0:depth]
        for start in range(0, hidden_width, step_f):
            block = pl.ds(start, step_f)
            gate = jnp.dot(inputs, gw[0, :, block], preferred_element_type=jnp.float32)
            up = jnp.dot(inputs, uw[0, :, block], preferred_element_type=jnp.float32)
            act[:, block] = (gate / (1.0 + jnp.exp(-gate)) * up).astype(jnp.bfloat16)
        for j in range(seqs):
            block = pl.ds(j * cols, cols)
            product = jnp.dot(act[...], dw[0, :, block], preferred_element_type=jnp.float32)
            y[role, :, block] = (product * share).astype(jnp.bfloat16)
            if j % (seqs // 2) == seqs // 2 - 1:
                yc(i, 1, role, j // (seqs // 2)).start()
                yc(i, 0, role, j // (seqs // 2)).start()

        return carry

    lax.fori_loop(0, roles, one_block, 0)
    for h in range(2):
        pass_core(3, h)
    for h in range(2):
        pass_core(0, h)
    for h in range(2):
        settle(1, 0, h)
    for h in range(2):
        settle(3, 1, h)
    for h in range(2):
        block = pl.ds(h * half, half)
        second = summed(2, h)
        yz(1, h).wait_recv()
        y[role_of(2), aligned(s, rows), block] = (
            second + y_role[1, :, block].astype(jnp.float32)
        ).astype(jnp.bfloat16)
        yz(2, h).start()
    for h in range(2):
        block = pl.ds(h * half, half)
        total = hid[:, block] + summed(0, h)
        for kind in (0, 2):
            yz(kind, h).wait_recv()
            total = total + y_role[kind, :, block].astype(jnp.float32)
        out_ref[0, :, block] = total.astype(out_ref.dtype)

    for off in offs:
        for t in range(2):
            kv1(t, off).wait_send()
    for kind in range(3):
        for j in range(seqs):
            pr(j, kind).wait_send()
        tz(kind, r, role_of(1)).wait_send()
        for h in range(2):
            yz(kind, h).wait_send()
        for t in range(2):
            kv2(t, kind, s, mate).wait_send()
    wo_own(s).wait_send()
    for c in range(chunks):
        wo_x(s, c).wait_send()
        wo_y(g, c).wait_send()
        for path in range(2):
            wo_mate(s, g, c, path).wait_send()
    for i in range(roles):
        tx(i, s, r).wait_send()
        for path in range(2):
            yx(i, r, path).wait_send()
            tc(i, path, s, r).wait_send()
            for h in range(2):
                yc(i, path, r, h).wait_send()


def fused(
    query_rows,
    encoded_key_rows,
    value_matrix_rows,
    output_weight,
    residual,
    norm_gain,
    route_experts,
    route_gates,
    gate_weight,
    up_weight,
    down_weight,
):
    seqs, roles = lax.axis_size("seq"), lax.axis_size("role")
    batch, rows, width = query_rows.shape
    depth, cols = residual.shape[2], output_weight.shape[1]
    hidden_width = gate_weight.shape[2]
    full = rows * seqs
    bf16, f32 = jnp.bfloat16, jnp.float32
    gain = norm_gain.reshape(1, depth)
    route_experts = route_experts.transpose(0, 2, 1)
    route_gates = route_gates.transpose(0, 2, 1)
    vmem = [
        pltpu.VMEM(query_rows.shape, bf16),
        pltpu.VMEM((2, batch, full, HEAD_WIDTH), bf16),
        pltpu.VMEM((seqs, width, cols), bf16),
        pltpu.VMEM(residual.shape, bf16),
        pltpu.VMEM(gain.shape, f32),
        pltpu.VMEM(route_experts.shape, jnp.int32),
        pltpu.VMEM(route_gates.shape, f32),
        pltpu.VMEM(gate_weight.shape, bf16),
        pltpu.VMEM(up_weight.shape, bf16),
        pltpu.VMEM(down_weight.shape, bf16),
        pltpu.VMEM((batch * rows, width), bf16),
        pltpu.VMEM((seqs, batch * rows, cols), bf16),
        pltpu.VMEM((seqs, 3, rows, cols), bf16),
        pltpu.VMEM((rows, depth), f32),
        pltpu.VMEM((roles, full, depth + LANES), bf16),
        pltpu.VMEM((full, hidden_width), bf16),
        pltpu.VMEM((roles, full, depth), bf16),
        pltpu.VMEM((roles, 2, rows, depth), bf16),
        pltpu.VMEM((roles, rows, depth), bf16),
        pltpu.VMEM((3, rows, depth), bf16),
    ]
    dma = pltpu.SemaphoreType.DMA
    counts = [(2, roles)] * 2 + [(2, 3)] * 2 + [(9,)] * 2 + [(4,)] * 4 + [(seqs, 3)] * 2
    counts += [(3,)] * 2 + [(roles,)] * 2 + [(roles, 2)] * 2 + [(roles, 4)] * 2
    counts += [(roles, 2)] * 2 + [(3, 2)] * 2
    return pl.pallas_call(
        partial(layer_kernel, roles, seqs),
        out_shape=jax.ShapeDtypeStruct(residual.shape, bf16),
        in_specs=[pl.BlockSpec(memory_space=pl.ANY)] * 11,
        out_specs=pl.BlockSpec(memory_space=pltpu.VMEM),
        scratch_shapes=vmem + [dma((9,)), dma((2,))] + [dma(count) for count in counts],
        compiler_params=pltpu.CompilerParams(
            collective_id=0, has_side_effects=True, vmem_limit_bytes=60 * 1024 * 1024
        ),
    )(
        query_rows,
        encoded_key_rows,
        value_matrix_rows,
        output_weight,
        residual,
        gain,
        route_experts,
        route_gates,
        gate_weight,
        up_weight,
        down_weight,
    )


def solution(mesh):
    square = mesh.shape["seq"] == 4 and mesh.shape["role"] == 4 and mesh.shape["groups"] == 2
    body = fused if square else shards
    placed = (
        P("groups", "seq", "role"),
        P("groups", ("seq", "role"), None),
        P("groups", ("seq", "role"), None),
        P("role", "seq"),
        P(("groups", "role"), "seq", None),
        P(),
        P(("groups", "role"), "seq", None),
        P(("groups", "role"), "seq", None),
        P(("seq", "role"), None, None),
        P(("seq", "role"), None, None),
        P(("seq", "role"), None, None),
    )
    return jax.shard_map(
        body,
        mesh=mesh,
        in_specs=placed,
        out_specs=P(("groups", "role"), "seq", None),
        check_vma=False,
    )
```
